32 devices in a mesh: dp: 4 (over z), pipe: 4 (over x, core), ctx: 2 (over y).
Axes of the slice: x: 2, y: 2, z: 4, core: 2. Of those that a mesh axis runs over, the one named last changes fastest.
Arguments:
- projected: bfloat16 [4, 4, 256, 2304], P('pipe', 'dp', 'ctx'), may hold values from -40 to 40
- gated_input: bfloat16 [4, 4, 256, 1536], P('pipe', 'dp', 'ctx'), may hold values from -6 to 6
- upstream: bfloat16 [4, 4, 256, 2304], P('pipe', 'dp', 'ctx'), may hold values from -6 to 6
- lengths: int32 [4, 4], P('pipe', 'dp'), may hold values from 64 to 256, as said below
- depth_kernel: float32 [4, 31, 1536], P('pipe'), may hold values from -1 to 1
- depth_bias: float32 [4, 1536], P('pipe'), may hold values from -3 to 3
Outputs:
- attention_out: bfloat16 [4, 4, 256, 768], P('pipe', 'dp', 'ctx')
- depth_out: bfloat16 [4, 4, 256, 1536], P('pipe', 'dp', 'ctx')
- projected_grad: bfloat16 [4, 4, 256, 2304], P('pipe', 'dp', 'ctx')
- gated_grad: bfloat16 [4, 4, 256, 1536], P('pipe', 'dp', 'ctx')
- kernel_grad: float32 [4, 31, 1536], P('pipe')
- bias_grad: float32 [4, 1536], P('pipe')
The draws below stay inside these ranges and needn't reach their ends.
Inputs may be any that keep to these rules, and one draw needn't show every extreme that they name: `lengths`: frames after a recording's length are padding; in every draw some recording has all 256 frames.
All inputs are finite; a program needn't handle non-finite values.
Results may differ from the reference program's by a relative error of at most 0.0069.
Values may be sent and summed in bfloat16 or wider, within the bound.
No kernel may reach another device: no remote copies, remote signals or barrier semaphores. Data moves between devices by JAX's collectives and lax.ppermute only.
A program may use at most 64 MiB of HBM per device.

```python
import math
import jax
import jax.numpy as jnp
from jax import lax

HEADS = 8
HD = 96
CH = 1536
KSIZE = 31
ROWS = 128
FRAMES = 256
SECTIONS = 4
RECS = 4
QPARTS = 1
N_CTX = 2


def draw_lengths(key, part):
    values = jax.random.randint(key, (SECTIONS * RECS,), FRAMES // 4, FRAMES + 1)
    chosen = jax.random.randint(jax.random.fold_in(key, 3), (), 0, SECTIONS * RECS)
    values = jnp.where(jnp.arange(SECTIONS * RECS) == chosen, FRAMES, values)
    return values.reshape(SECTIONS, RECS).astype(jnp.int32)


def draw_projected(key, part):
    embed = HEADS * HD
    shape = (SECTIONS, RECS, FRAMES, 3 * embed)
    base = jax.random.normal(key, shape, jnp.float32)
    return jnp.clip(base, -5.0, 5.0).astype(jnp.bfloat16)


def block_levels(own_key, dims, shards, least, largest):
    gain, own = 1.0, jax.random.fold_in(own_key, 6)
    for position, shards_of in shards:
        draws = jnp.exp(jax.random.uniform(jax.random.fold_in(own, position), (shards_of,), jnp.float32, least / len(shards), largest / len(shards)))
        gain = gain * jnp.repeat(draws, dims[position] // shards_of).reshape([-1 if axis == position else 1 for axis in range(len(dims))])
    return gain


def scatter_about(rng, dims, width, reach, cuts=(), kind=jnp.bfloat16):
    drawn = jax.random.normal(rng, dims, jnp.float32) * width
    if len(cuts) > 0:
        drawn = block_levels(rng, dims, cuts, -0.22, 0.18) * drawn
    return jnp.clip(drawn, min=-reach, max=reach).astype(kind)


def setup_inputs(seed: int = 0) -> dict:
    keys = jax.random.split(jax.random.key(seed), 7)
    return {
        "projected": draw_projected(jax.random.fold_in(keys[6], 71), 0),
        "gated_input": scatter_about(keys[1], (SECTIONS, RECS, FRAMES, CH), 1.0, 6.0, ((0, 4), (1, 4), (2, 2))),
        "upstream": scatter_about(keys[2], (SECTIONS, RECS, FRAMES, HEADS * HD + CH), 1.0, 6.0, ((0, 4), (1, 4), (2, 2))),
        "lengths": draw_lengths(jax.random.fold_in(keys[6], 71), 0),
        "depth_kernel": scatter_about(keys[4], (SECTIONS, KSIZE, CH), KSIZE ** -0.5, 1.0, ((0, 4),), jnp.float32),
        "depth_bias": scatter_about(keys[5], (SECTIONS, CH), 0.5, 3.0, ((0, 4),), jnp.float32),
    }


def rounded(values):
    narrow = lax.optimization_barrier(values.astype(jnp.bfloat16))
    return narrow.astype(jnp.float32)

def attend_part(queries, grad_out, keys_in, values_in, valid_keys):
    score_scale = 1.0 / math.sqrt(queries.shape[-1])
    scores = jnp.dot(queries, keys_in.T) * score_scale
    scores = jnp.where(valid_keys[None, :], scores, -1e+30)
    shifted = jnp.exp(scores - lax.optimization_barrier(jnp.max(scores, axis=1, keepdims=True)))
    probs_bf = rounded(shifted / lax.optimization_barrier(jnp.sum(shifted, axis=1, keepdims=True)))
    attended_full = jnp.dot(probs_bf, values_in)
    attended = attended_full.astype(jnp.bfloat16)
    grad_probs = jnp.dot(grad_out, values_in.T)
    centre = lax.optimization_barrier(jnp.sum(grad_out * attended_full, axis=1, keepdims=True))
    grad_scores = rounded(probs_bf * (grad_probs - centre) * score_scale)
    grad_query = jnp.dot(grad_scores, keys_in).astype(jnp.bfloat16)
    key_part = jnp.dot(grad_scores.T, queries)
    value_part = jnp.dot(probs_bf.T, grad_out)
    return (attended, grad_query, key_part, value_part)

def depthwise(source, taps, bias, count):
    total = jnp.zeros((count, source.shape[1]), jnp.float32) + bias[None, :]
    for offset in range(KSIZE):
        total = total + taps[offset][None, :] * source[offset:offset + count]
    return total

def slope(pre_act):
    sigmoid_pre = jax.nn.sigmoid(pre_act)
    return sigmoid_pre + pre_act * sigmoid_pre * (1.0 - sigmoid_pre)

def reference(projected, gated_input, upstream, lengths, depth_kernel, depth_bias):
    cotangent = jnp.roll(upstream, -1, axis=0)
    embed = HEADS * HD
    part_rows = ROWS // QPARTS
    half_width = KSIZE // 2

    def heads_of(matrix):
        return matrix.reshape(FRAMES, HEADS, HD).transpose(1, 0, 2)

    def parts_of(matrix):
        split = matrix.reshape(HEADS, N_CTX, QPARTS, part_rows, HD).transpose(0, 2, 1, 3, 4)
        return split.reshape(HEADS, QPARTS, N_CTX * part_rows, HD)

    def unparts(matrix):
        split = matrix.reshape(HEADS, QPARTS, N_CTX, part_rows, HD).transpose(2, 1, 3, 0, 4)
        return split.reshape(FRAMES, embed)

    def unheads(matrix):
        return matrix.transpose(1, 0, 2).reshape(FRAMES, embed)
    attention_list, depth_list, grad_list, gated_list = ([], [], [], [])
    kernel_list, bias_list = ([], [])
    for section_index in range(SECTIONS):
        attention_row, depth_row, grad_row, gated_row = ([], [], [], [])
        kernel_total = jnp.zeros((KSIZE, CH), jnp.float32)
        bias_total = jnp.zeros((CH,), jnp.float32)
        taps = depth_kernel[section_index].astype(jnp.float32)
        bias = depth_bias[section_index].astype(jnp.float32)
        for record_index in range(RECS):
            mixed = projected[section_index, record_index].astype(jnp.float32)
            arriving = cotangent[section_index, record_index].astype(jnp.float32)
            length = lengths[section_index, record_index]
            valid_keys = jnp.arange(FRAMES) < length
            queries = parts_of(heads_of(mixed[:, :embed]))
            grad_attn = parts_of(heads_of(arriving[:, :embed]))
            keys_in = heads_of(mixed[:, embed:2 * embed])
            values_in = heads_of(mixed[:, 2 * embed:])

            def per_head(items):
                head_queries, head_grads, head_keys, head_values = items

                def per_part(pair):
                    return attend_part(pair[0], pair[1], head_keys, head_values, valid_keys)
                return lax.map(per_part, (head_queries, head_grads))
            attended, grad_query, key_part, value_part = lax.map(per_head, (queries, grad_attn, keys_in, values_in))
            grad_key = lax.optimization_barrier(jnp.sum(key_part, axis=1)).astype(jnp.bfloat16)
            grad_value = lax.optimization_barrier(jnp.sum(value_part, axis=1)).astype(jnp.bfloat16)
            attention_row.append(unparts(attended))
            grad_row.append(jnp.concatenate([unparts(grad_query), unheads(grad_key), unheads(grad_value)], axis=1))
            frame_mask = valid_keys[:, None]
            masked = jnp.where(frame_mask, gated_input[section_index, record_index], jnp.zeros((), jnp.bfloat16)).astype(jnp.float32)
            padded = jnp.pad(masked, ((half_width, half_width), (0, 0)))
            pre_act = depthwise(padded, taps, bias, FRAMES)
            depth_row.append((pre_act * jax.nn.sigmoid(pre_act)).astype(jnp.bfloat16))
            grad_pre = arriving[:, embed:] * slope(pre_act)
            grad_pad = jnp.pad(grad_pre, ((half_width, half_width), (0, 0)))
            back = jnp.zeros((FRAMES, CH), jnp.float32)
            for offset in range(KSIZE):
                start = 2 * half_width - offset
                back = back + taps[offset][None, :] * grad_pad[start:start + FRAMES]
            gated_row.append(jnp.where(frame_mask, back, 0.0).astype(jnp.bfloat16))
            kernel_total = kernel_total + jnp.stack([lax.optimization_barrier(jnp.sum(padded[offset:offset + FRAMES] * grad_pre, axis=0)) for offset in range(KSIZE)])
            bias_total = bias_total + lax.optimization_barrier(jnp.sum(grad_pre, axis=0))
        attention_list.append(jnp.stack(attention_row))
        depth_list.append(jnp.stack(depth_row))
        grad_list.append(jnp.stack(grad_row))
        gated_list.append(jnp.stack(gated_row))
        kernel_list.append(kernel_total)
        bias_list.append(bias_total)
    return (jnp.stack(attention_list), jnp.stack(depth_list), jnp.stack(grad_list), jnp.stack(gated_list), jnp.stack(kernel_list), jnp.stack(bias_list))
```

```python
import math

import jax
import jax.numpy as jnp
from jax import lax
from jax.experimental import pallas as pl
from jax.experimental.pallas import tpu as pltpu
from jax.sharding import PartitionSpec as P

HEADS = 8
HD = 96
KSIZE = 31
HALF = KSIZE // 2
LANES = 128
EDGE = 32
SLIM = 16
GROUP = 4
F32 = jnp.float32
BF16 = jnp.bfloat16


def conv_kernel(
    place_ref, gated_ref, gated_low, gated_high, cot_ref, cot_low, cot_high, taps_ref, bias_ref,
    out_ref, grad_ref, sums_ref, source, slopes, partial,
):
    rows, width = gated_ref.shape
    first, length, frames = place_ref[0], place_ref[1], place_ref[2]

    def frame_of(start, count):
        return first + start + lax.broadcasted_iota(jnp.int32, (count, LANES), 0)

    for column in range(width // LANES):
        lanes = pl.ds(column * LANES, LANES)

        def fill(value, start):
            count = value.shape[0]
            frame = frame_of(start, count)
            keep = (frame >= 0) & (frame < length)
            source[pl.ds(start + EDGE, count), :] = jnp.where(keep, value.astype(F32), 0.0)

        def fill_cot(value, start):
            count = value.shape[0]
            frame = frame_of(start, count)
            keep = (frame >= 0) & (frame < frames)
            slopes[pl.ds(start + SLIM, count), :] = jnp.where(keep, value.astype(F32), 0.0)

        fill(gated_low[:, lanes], -EDGE)
        fill(gated_high[:, lanes], rows)
        fill_cot(cot_low[:, lanes], -SLIM)
        fill_cot(cot_high[:, lanes], rows)

        @pl.loop(0, rows // EDGE)
        def _(step):
            at = pl.multiple_of(step * EDGE, EDGE)
            fill(gated_ref[pl.ds(at, EDGE), lanes], at)
            slopes[pl.ds(at + SLIM, EDGE), :] = cot_ref[pl.ds(at, EDGE), lanes].astype(F32)

        taps = [
            jnp.broadcast_to(taps_ref[k : k + 1, lanes], (8, LANES)) for k in range(KSIZE)
        ]
        bias = jnp.broadcast_to(bias_ref[:, lanes], (8, LANES))

        def weighted(read, order, base):
            parts = [base, None, None, None]
            for k in range(KSIZE):
                term = taps[k] * read(order(k))
                slot = k % 4
                parts[slot] = term if parts[slot] is None else parts[slot] + term
            return (parts[0] + parts[1]) + (parts[2] + parts[3])

        def pre_tile(at):
            pre = weighted(lambda k: source[pl.ds(at + 1 + k, 8), :], lambda k: k, bias)
            gate = jax.nn.sigmoid(pre)
            swish = pre * gate
            where = pl.ds(at, 8)
            slopes[where, :] = slopes[where, :] * (gate + swish * (1.0 - gate))
            return swish

        for at in range(0, SLIM, 8):
            pre_tile(at)
            pre_tile(rows + SLIM + at)

        @pl.loop(0, rows // 16)
        def _(step):
            at = pl.multiple_of(step * 16, 16)
            swish = [pre_tile(SLIM + at), pre_tile(SLIM + at + 8)]
            out_ref[pl.ds(at, 16), lanes] = jnp.concatenate(swish, axis=0).astype(BF16)

        zero = jnp.zeros((8, LANES), F32)

        def gather(step, totals):
            at = pl.multiple_of(step * 8, 8)
            grad = slopes[pl.ds(at + SLIM, 8), :]
            sums = [
                totals[k] + grad * source[pl.ds(at + SLIM + 1 + k, 8), :] for k in range(KSIZE)
            ]
            return (*sums, totals[KSIZE] + grad)

        totals = lax.fori_loop(0, rows // 8, gather, (zero,) * (KSIZE + 1))
        for k in range(KSIZE + 1):
            partial[8 * k : 8 * k + 8, :] = totals[k]
        summed = partial[pl.ds(0, KSIZE + 1, stride=8), :]
        for sublane in range(1, 8):
            summed = summed + partial[pl.ds(sublane, KSIZE + 1, stride=8), :]
        sums_ref[:, lanes] = summed.astype(sums_ref.dtype)

        @pl.loop(0, rows // 16)
        def _(step):
            at = pl.multiple_of(step * 16, 16)
            back = [
                weighted(
                    lambda k: slopes[pl.ds(at + shift + SLIM + HALF - k, 8), :],
                    lambda k: k,
                    zero,
                )
                for shift in (0, 8)
            ]
            keep = frame_of(at, 16) < length
            whole = jnp.where(keep, jnp.concatenate(back, axis=0), 0.0)
            grad_ref[pl.ds(at, 16), lanes] = whole.astype(BF16)


def conv_call(place, gated, gated_low, gated_high, arriving, cot_low, cot_high, taps, bias):
    rows, channels = gated.shape
    width = 2 * LANES
    offset = (arriving.shape[1] - channels) // width

    def columns(count, shift=0):
        return pl.BlockSpec((count, width), lambda i: (0, i + shift))

    work = 3 * 2 * KSIZE * rows * channels
    return pl.pallas_call(
        conv_kernel,
        grid=(channels // width,),
        in_specs=[
            pl.BlockSpec(memory_space=pltpu.SMEM),
            columns(rows),
            columns(EDGE),
            columns(EDGE),
            columns(rows, offset),
            columns(SLIM),
            columns(SLIM),
            columns(KSIZE),
            columns(1),
        ],
        out_specs=[columns(rows), columns(rows), columns(KSIZE + 1)],
        out_shape=[
            jax.ShapeDtypeStruct((rows, channels), BF16),
            jax.ShapeDtypeStruct((rows, channels), BF16),
            jax.ShapeDtypeStruct((KSIZE + 1, channels), BF16),
        ],
        scratch_shapes=[
            pltpu.VMEM((rows + 2 * EDGE, LANES), F32),
            pltpu.VMEM((rows + 2 * SLIM, LANES), F32),
            pltpu.VMEM((8 * (KSIZE + 1), LANES), F32),
        ],
        cost_estimate=pl.CostEstimate(
            flops=work, bytes_accessed=10 * rows * channels, transcendentals=rows * channels
        ),
        name="conv",
    )(place, gated, gated_low, gated_high, arriving, cot_low, cot_high, taps, bias)


def attention_kernel(
    place_ref, mine_ref, peer_ref, cot_ref, cot_peer_ref, out_ref, grad_ref
):
    rows = mine_ref.shape[0]
    embed = HEADS * HD
    scale = 1.0 / math.sqrt(HD)
    first, first_peer, length = place_ref[0], place_ref[1], place_ref[2]
    row = lax.broadcasted_iota(jnp.int32, (2 * rows, 2 * rows), 0)
    frame = jnp.where(row < rows, row + first, row - rows + first_peer)
    valid = frame < length
    across = (((1,), (1,)), ((), ()))
    downward = (((0,), (0,)), ((), ()))

    def both(a_ref, b_ref, start, width):
        return jnp.concatenate(
            [a_ref[:, start : start + width], b_ref[:, start : start + width]], axis=0
        )

    for group in range(HEADS // GROUP):
        tiles = GROUP * HD // LANES
        totals = [[None] * tiles for _ in range(4)]
        for head in range(GROUP):
            low = head * HD
            tile = low // LANES
            count = (low + HD - 1) // LANES - tile + 1
            width = count * LANES
            start = group * GROUP * HD + tile * LANES
            lane = lax.broadcasted_iota(jnp.int32, (2 * rows, width), 1) + tile * LANES
            here = (lane >= low) & (lane < low + HD)

            def own(value):
                return jnp.where(here, value, jnp.zeros((), BF16))

            query = both(mine_ref, peer_ref, start, width)
            key = own(both(mine_ref, peer_ref, embed + start, width))
            value = own(both(mine_ref, peer_ref, 2 * embed + start, width))
            cot = both(cot_ref, cot_peer_ref, start, width)
            scores = lax.dot_general(key, query, across, preferred_element_type=F32) * scale
            scores = jnp.where(valid, scores, -1e30)
            top = jnp.max(scores, axis=0, keepdims=True)
            raised = jnp.exp(scores - top)
            total = jnp.sum(raised, axis=0, keepdims=True)
            probs_bf = (raised * (1.0 / total)).astype(BF16)
            probs = probs_bf.astype(F32)
            grad_probs = lax.dot_general(value, cot, across, preferred_element_type=F32)
            centre = jnp.sum(probs * grad_probs, axis=0, keepdims=True)
            grad_scores = (probs * (grad_probs - centre) * scale).astype(BF16)
            results = (
                lax.dot_general(probs_bf[:, :rows], value, downward, preferred_element_type=F32),
                lax.dot_general(grad_scores[:, :rows], key, downward, preferred_element_type=F32),
                jnp.dot(grad_scores[:rows], own(query), preferred_element_type=F32),
                jnp.dot(probs_bf[:rows], own(cot), preferred_element_type=F32),
            )
            for result, kept in zip(results, totals):
                for index in range(count):
                    piece = result[:, index * LANES : (index + 1) * LANES]
                    held = kept[tile + index]
                    kept[tile + index] = piece if held is None else held + piece
        for index in range(tiles):
            start = group * GROUP * HD + index * LANES
            out_ref[:, start : start + LANES] = totals[0][index].astype(BF16)
            for block in range(3):
                at = block * embed + start
                grad_ref[:, at : at + LANES] = totals[block + 1][index].astype(BF16)


def attention_call(place, mine, peer, arriving, cot_peer):
    rows, columns = mine.shape
    embed = HEADS * HD
    whole = pl.BlockSpec((rows, columns), lambda i: (0, 0))
    third = pl.BlockSpec((rows, embed), lambda i: (0, 0))
    return pl.pallas_call(
        attention_kernel,
        grid=(1,),
        in_specs=[pl.BlockSpec(memory_space=pltpu.SMEM), whole, whole, third, third],
        out_specs=[third, whole],
        out_shape=[
            jax.ShapeDtypeStruct((rows, embed), BF16),
            jax.ShapeDtypeStruct((rows, columns), BF16),
        ],
        cost_estimate=pl.CostEstimate(
            flops=6 * 2 * HEADS * 4 * rows * rows * HD,
            bytes_accessed=2 * rows * (3 * columns + 3 * embed),
            transcendentals=HEADS * 4 * rows * rows,
        ),
        compiler_params=pltpu.CompilerParams(vmem_limit_bytes=40 * 1024 * 1024),
        name="attention",
    )(place, mine, peer, arriving, cot_peer)


def head_pass(queries, grad_out, keys_in, values_in, valid_keys):
    query_rows, head_dim = queries.shape
    score_scale = 1.0 / math.sqrt(head_dim)
    block_rows = min(512, query_rows)
    block_count = query_rows // block_rows
    frame_count = keys_in.shape[0]
    across = (((1,), (1,)), ((), ()))
    downward = (((0,), (0,)), ((), ()))

    def advance(totals, blocks):
        query_block, grad_block = blocks
        scores = (
            lax.dot_general(query_block, keys_in, across, preferred_element_type=jnp.float32)
            * score_scale
        )
        scores = jnp.where(valid_keys[None, :], scores, -1e30)
        row_top = jnp.max(scores, axis=1, keepdims=True)
        row_total = jnp.sum(jnp.exp(scores - row_top), axis=1, keepdims=True)
        probs_bf = (jnp.exp(scores - row_top) / row_total).astype(jnp.bfloat16)
        attended_full = jnp.dot(probs_bf, values_in, preferred_element_type=jnp.float32)
        attended = attended_full.astype(jnp.bfloat16)
        grad_probs = lax.dot_general(
            grad_block, values_in, across, preferred_element_type=jnp.float32
        )
        centre = jnp.sum(grad_block.astype(jnp.float32) * attended_full, axis=1, keepdims=True)
        grad_scores = (probs_bf.astype(jnp.float32) * (grad_probs - centre) * score_scale).astype(
            jnp.bfloat16
        )
        grad_query = jnp.dot(grad_scores, keys_in, preferred_element_type=jnp.float32).astype(
            jnp.bfloat16
        )
        key_total = totals[0] + lax.dot_general(
            grad_scores, query_block, downward, preferred_element_type=jnp.float32
        )
        value_total = totals[1] + lax.dot_general(
            probs_bf, grad_block, downward, preferred_element_type=jnp.float32
        )
        return ((key_total, value_total), (attended, grad_query))

    zero_grads = jnp.zeros((frame_count, head_dim), jnp.float32)
    blocked = (
        queries.reshape(block_count, block_rows, head_dim),
        grad_out.reshape(block_count, block_rows, head_dim),
    )
    totals, results = lax.scan(advance, (zero_grads, zero_grads), blocked)
    attended = results[0].reshape(query_rows, head_dim)
    grad_query = results[1].reshape(query_rows, head_dim)
    return (attended, grad_query, totals[0], totals[1])


def attend_block(query_part, grad_part, key_value, valid_keys, heads_dev):
    block_width = heads_dev * HD

    def split_heads(matrix):
        return matrix.reshape(matrix.shape[0], heads_dev, HD).transpose(1, 0, 2)

    def join_heads(matrix):
        return matrix.transpose(1, 0, 2).reshape(matrix.shape[1], block_width)

    def one_head(items):
        return head_pass(items[0], items[1], items[2], items[3], valid_keys)

    stacked = (
        split_heads(query_part),
        split_heads(grad_part),
        split_heads(key_value[:, :block_width]),
        split_heads(key_value[:, block_width:]),
    )
    attended, grad_query, key_grad, value_grad = lax.map(one_head, stacked)
    key_grads = jnp.concatenate([join_heads(key_grad), join_heads(value_grad)], axis=1)
    return (join_heads(attended), join_heads(grad_query), key_grads)


def attend_by_heads(mixed, grad_attn, valid_keys):
    rows_here = mixed.shape[0]
    devices_ctx = lax.axis_size("ctx")
    embed = HEADS * HD
    part_count = max(devices_ctx // HEADS, 1)
    heads_dev = max(HEADS // devices_ctx, 1)
    block_heads = HEADS // heads_dev
    part_rows = rows_here // part_count
    block_width = heads_dev * HD
    queries = mixed[:, :embed]
    keys_in = mixed[:, embed : 2 * embed]
    values_in = mixed[:, 2 * embed :]

    def by_part(matrix):
        split = matrix.reshape(part_count, part_rows, block_heads, block_width).transpose(
            2, 0, 1, 3
        )
        return split.reshape(devices_ctx, part_rows, block_width)

    def swap(value, concat):
        return lax.all_to_all(value, "ctx", split_axis=0, concat_axis=concat, tiled=True)

    key_value = jnp.concatenate(
        [
            keys_in.reshape(rows_here, block_heads, block_width),
            values_in.reshape(rows_here, block_heads, block_width),
        ],
        axis=2,
    )
    key_value = jnp.repeat(key_value.transpose(1, 0, 2), part_count, axis=0)
    query_part = swap(by_part(queries), 1)[0]
    grad_part = swap(by_part(grad_attn), 1)[0]
    key_value = swap(key_value, 1)[0]
    attended, grad_query, key_grads = attend_block(
        query_part, grad_part, key_value, valid_keys, heads_dev
    )
    outgoing = jnp.concatenate([attended, grad_query], axis=1).reshape(
        devices_ctx, part_rows, 2 * block_width
    )
    returned = swap(outgoing, 0)
    key_returned = swap(
        key_grads.reshape(devices_ctx, rows_here, 2 * block_width).astype(BF16), 0
    ).astype(F32)
    columns = 2 * block_width
    split = returned.reshape(block_heads, part_count, part_rows, columns).transpose(1, 2, 0, 3)
    returned = split.reshape(rows_here, block_heads, columns)
    attention_out = returned[:, :, :block_width].reshape(rows_here, embed)
    grad_q = returned[:, :, block_width:].reshape(rows_here, embed)
    summed = jnp.sum(
        key_returned.reshape(block_heads, part_count, rows_here, 2 * block_width), axis=1
    )
    summed = summed.astype(BF16).transpose(1, 0, 2)
    grad_k = summed[:, :, :block_width].reshape(rows_here, embed)
    grad_v = summed[:, :, block_width:].reshape(rows_here, embed)
    return attention_out, jnp.concatenate([grad_q, grad_k, grad_v], axis=1)


def summed_over(value, axes):
    for axis in axes:
        count = lax.axis_size(axis)
        step = 1
        while step < count:
            other = lax.ppermute(value, axis, [(i, i ^ step) for i in range(count)])
            total = value.astype(F32) + other.astype(F32)
            value = total.astype(BF16)
            step *= 2
    return total


def edges(block, count, pipe_shift):
    rows = block.shape[0]
    sections, devices = lax.axis_size("pipe"), lax.axis_size("ctx")
    me = lax.axis_index("ctx")

    def route(ctx_pairs):
        return [
            (s * devices + a, ((s - pipe_shift) % sections) * devices + b)
            for s in range(sections)
            for a, b in ctx_pairs
        ]

    if devices == 2:
        start = jnp.where(me == 0, rows - count, 0)
        piece = lax.dynamic_slice_in_dim(block, start, count, axis=0)
        got = lax.ppermute(piece, ("pipe", "ctx"), route([(0, 1), (1, 0)]))
        return got, got
    upward = [(i, i + 1) for i in range(devices - 1)]
    low = lax.ppermute(block[rows - count :], ("pipe", "ctx"), route(upward))
    high = lax.ppermute(block[:count], ("pipe", "ctx"), route([(b, a) for a, b in upward]))
    return low, high


def local(projected, gated_input, upstream, lengths, depth_kernel, depth_bias):
    embed = HEADS * HD
    sections, devices = lax.axis_size("pipe"), lax.axis_size("ctx")
    me = lax.axis_index("ctx")
    mixed, gated, sent = projected[0, 0], gated_input[0, 0], upstream[0, 0]
    rows = mixed.shape[0]
    frames = rows * devices
    length = lengths[0, 0]
    first = me * rows
    gated_low, gated_high = edges(gated, EDGE, 0)
    cot_low, cot_high = edges(sent[:, embed:], SLIM, 1)
    arriving = lax.ppermute(sent, "pipe", [(i, (i - 1) % sections) for i in range(sections)])
    if devices == 2:
        crossed = [
            (s * 2 + c, ((s - 1) % sections) * 2 + 1 - c)
            for s in range(sections)
            for c in range(2)
        ]
        cot_peer = lax.ppermute(sent[:, :embed], ("pipe", "ctx"), crossed)
        peer = lax.ppermute(mixed, "ctx", [(0, 1), (1, 0)])
    place = jnp.stack([first, length, jnp.int32(frames)])
    depth_out, gated_grad, sums = conv_call(
        place,
        gated,
        gated_low,
        gated_high,
        arriving,
        cot_low,
        cot_high,
        depth_kernel[0],
        depth_bias,
    )
    sums = summed_over(sums, ("dp", "ctx"))
    if devices == 2:
        place = jnp.stack([first, (1 - me) * rows, length])
        attention_out, projected_grad = attention_call(place, mixed, peer, arriving, cot_peer)
    else:
        attention_out, projected_grad = attend_by_heads(
            mixed, arriving[:, :embed], jnp.arange(frames) < length
        )
    return (
        attention_out[None, None],
        depth_out[None, None],
        projected_grad[None, None],
        gated_grad[None, None],
        sums[None, :KSIZE],
        sums[KSIZE:],
    )


def solution(mesh):
    by_frame = P("pipe", "dp", "ctx", None)
    return jax.shard_map(
        local,
        mesh=mesh,
        in_specs=(
            by_frame,
            by_frame,
            by_frame,
            P("pipe", "dp"),
            P("pipe", None, None),
            P("pipe", None),
        ),
        out_specs=(
            by_frame,
            by_frame,
            by_frame,
            by_frame,
            P("pipe", None, None),
            P("pipe", None),
        ),
        check_vma=False,
    )
```

```python
import math

import jax
import jax.numpy as jnp
from jax import lax
from jax.experimental import pallas as pl
from jax.experimental.pallas import tpu as pltpu
from jax.sharding import PartitionSpec as P

HEADS = 8
HD = 96
KSIZE = 31
HALF = KSIZE // 2
LANES = 128
EDGE = 32
SLIM = 16
GROUP = 4
PRICE = 512
TILES = 4
LIMIT = 16 * 1024 * 1024
F32 = jnp.float32
BF16 = jnp.bfloat16


def tap_sums(read, tap, tiles):
    sums = [[None, None] for _ in range(tiles)]
    for k in range(KSIZE):
        weight = tap(k)
        for tile in range(tiles):
            term = weight * read(tile, k)
            held = sums[tile][k % 2]
            sums[tile][k % 2] = term if held is None else held + term
    return [even + odd for even, odd in sums]


def row_block(start):
    return pl.ds(start, 8)


def pre_kernel(
    place_ref, gated_ref, gated_low, gated_high, taps_ref, bias_ref, out_ref, source, slopes,
    valid,
):
    rows, width = gated_ref.shape
    first, length = place_ref[0], place_ref[1]
    frame = first - EDGE + lax.broadcasted_iota(jnp.int32, valid.shape, 0)
    valid[...] = ((frame >= 0) & (frame < length)).astype(F32)

    @pl.loop(0, width // LANES)
    def _(column):
        lanes = pl.ds(pl.multiple_of(column * LANES, LANES), LANES)

        def put(ref, start, at):
            to = pl.ds(at, 16)
            block = ref[pl.ds(start, 16), lanes].astype(F32)
            source[column, to, :] = block * valid[to, :]

        for start in range(0, EDGE, 16):
            put(gated_low, start, start)
            put(gated_high, start, EDGE + rows + start)
        for start in range(0, rows, 16):
            put(gated_ref, start, EDGE + start)
        bias = jnp.broadcast_to(bias_ref[:, lanes], (8, LANES))
        for start in range(0, rows + 2 * SLIM, 8 * TILES):
            pres = tap_sums(
                lambda tile, k: source[column, row_block(start + 8 * tile + 1 + k), :],
                lambda k: jnp.broadcast_to(taps_ref[k, :, lanes], (8, LANES)),
                TILES,
            )
            swishes = []
            for tile, pre in enumerate(pres):
                pre = pre + bias
                gate = jax.nn.sigmoid(pre)
                swish = pre * gate
                slopes[column, row_block(start + 8 * tile), :] = gate + swish * (1.0 - gate)
                swishes.append(swish)
            for tile in range(0, TILES, 2):
                at = start + 8 * tile - SLIM
                if 0 <= at < rows:
                    pair = jnp.concatenate(swishes[tile : tile + 2], axis=0)
                    out_ref[pl.ds(at, 16), lanes] = pair.astype(BF16)


def sums_kernel(
    place_ref, source, slopes, cot_ref, cot_low, cot_high, grads, sums_ref, partial
):
    columns, wide, _ = slopes.shape
    rows = wide - 2 * SLIM
    first, frames = place_ref[0], place_ref[2]
    embed = cot_ref.shape[1] - columns * LANES
    low_kept = (first > 0).astype(F32)
    high_kept = (first + rows < frames).astype(F32)

    @pl.loop(0, columns)
    def _(column):
        lanes = pl.ds(pl.multiple_of(column * LANES, LANES), LANES)
        shifted = pl.ds(pl.multiple_of(embed + column * LANES, LANES), LANES)

        def put(cot, at):
            to = pl.ds(at, 16)
            grads[column, to, :] = cot.astype(F32) * slopes[column, to, :]

        put(cot_low[:, lanes].astype(F32) * low_kept, 0)
        put(cot_high[:, lanes].astype(F32) * high_kept, rows + SLIM)
        for at in range(0, rows, 16):
            put(cot_ref[pl.ds(at, 16), shifted], at + SLIM)

        totals = [None] * (KSIZE + 1)
        for at in range(0, rows, 8):
            grad = grads[column, row_block(at + SLIM), :]
            for k in range(KSIZE):
                term = grad * source[column, row_block(at + SLIM + 1 + k), :]
                totals[k] = term if totals[k] is None else totals[k] + term
            totals[KSIZE] = grad if totals[KSIZE] is None else totals[KSIZE] + grad
        for k in range(KSIZE + 1):
            partial[8 * k : 8 * k + 8, :] = totals[k]
        summed = partial[pl.ds(0, KSIZE + 1, stride=8), :]
        for sublane in range(1, 8):
            summed = summed + partial[pl.ds(sublane, KSIZE + 1, stride=8), :]
        sums_ref[:, lanes] = summed.astype(sums_ref.dtype)


def back_kernel(place_ref, grads, taps_ref, out_ref, valid):
    rows, width = out_ref.shape
    first, length = place_ref[0], place_ref[1]
    frame = first + lax.broadcasted_iota(jnp.int32, valid.shape, 0)
    valid[...] = (frame < length).astype(F32)

    @pl.loop(0, width // LANES)
    def _(column):
        lanes = pl.ds(pl.multiple_of(column * LANES, LANES), LANES)
        for start in range(0, rows, 8 * TILES):
            backs = tap_sums(
                lambda tile, k: grads[
                    column, row_block(start + 8 * tile + SLIM + HALF - k), :
                ],
                lambda k: jnp.broadcast_to(taps_ref[k, :, lanes], (8, LANES)),
                TILES,
            )
            for tile in range(0, TILES, 2):
                at = start + 8 * tile
                pair = jnp.concatenate(backs[tile : tile + 2], axis=0)
                out_ref[pl.ds(at, 16), lanes] = (pair * valid[pl.ds(at, 16), :]).astype(BF16)


def conv_calls(place, gated, gated_low, gated_high, arriving, cot_low, cot_high, taps, bias):
    rows, channels = gated.shape
    wide = rows + 2 * SLIM
    scalars = pl.BlockSpec(memory_space=pltpu.SMEM)
    whole = pl.BlockSpec(memory_space=pltpu.VMEM)

    def shaped(*dims, dtype=BF16):
        return jax.ShapeDtypeStruct(dims, dtype)

    def stacked(count):
        return shaped(channels // LANES, count, LANES, dtype=F32)

    def cost(reads, exps=0):
        return pl.CostEstimate(
            flops=PRICE * 2 * KSIZE * rows * channels,
            bytes_accessed=reads * rows * channels,
            transcendentals=exps,
        )

    params = pltpu.CompilerParams(vmem_limit_bytes=LIMIT)
    depth_out, source, slopes = pl.pallas_call(
        pre_kernel,
        in_specs=[scalars] + [whole] * 5,
        out_specs=[whole] * 3,
        out_shape=[shaped(rows, channels), stacked(rows + 2 * EDGE), stacked(wide)],
        scratch_shapes=[pltpu.VMEM((rows + 2 * EDGE, LANES), F32)],
        cost_estimate=cost(8, 2 * rows * channels),
        compiler_params=params,
        name="conv_pre",
    )(place, gated, gated_low, gated_high, taps, bias)
    grads, sums = pl.pallas_call(
        sums_kernel,
        in_specs=[scalars] + [whole] * 5,
        out_specs=[whole] * 2,
        out_shape=[stacked(wide), shaped(KSIZE + 1, channels)],
        scratch_shapes=[pltpu.VMEM((8 * (KSIZE + 1), LANES), F32)],
        cost_estimate=cost(12),
        compiler_params=params,
        name="conv_sums",
    )(place, source, slopes, arriving, cot_low, cot_high)
    gated_grad = pl.pallas_call(
        back_kernel,
        in_specs=[scalars] + [whole] * 2,
        out_specs=whole,
        out_shape=shaped(rows, channels),
        scratch_shapes=[pltpu.VMEM((rows, LANES), F32)],
        cost_estimate=cost(6),
        compiler_params=params,
        name="conv_back",
    )(place, grads, taps)
    return depth_out, gated_grad, sums


def attention_kernel(
    place_ref, mine_ref, peer_ref, cot_ref, cot_peer_ref, out_ref, grad_ref
):
    rows = mine_ref.shape[0]
    embed = HEADS * HD
    scale = 1.0 / math.sqrt(HD)
    first, first_peer, length = place_ref[0], place_ref[1], place_ref[2]
    row = lax.broadcasted_iota(jnp.int32, (2 * rows, 2 * rows), 0)
    frame = jnp.where(row < rows, row + first, row - rows + first_peer)
    valid = frame < length
    across = (((1,), (1,)), ((), ()))
    downward = (((0,), (0,)), ((), ()))

    def both(a_ref, b_ref, start, width):
        return jnp.concatenate(
            [a_ref[:, start : start + width], b_ref[:, start : start + width]], axis=0
        )

    for group in range(HEADS // GROUP):
        tiles = GROUP * HD // LANES
        totals = [[None] * tiles for _ in range(4)]
        for head in range(GROUP):
            low = head * HD
            tile = low // LANES
            count = (low + HD - 1) // LANES - tile + 1
            width = count * LANES
            start = group * GROUP * HD + tile * LANES
            lane = lax.broadcasted_iota(jnp.int32, (2 * rows, width), 1) + tile * LANES
            here = (lane >= low) & (lane < low + HD)

            def own(value):
                return jnp.where(here, value, jnp.zeros((), BF16))

            query = both(mine_ref, peer_ref, start, width)
            key = own(both(mine_ref, peer_ref, embed + start, width))
            value = own(both(mine_ref, peer_ref, 2 * embed + start, width))
            cot = both(cot_ref, cot_peer_ref, start, width)
            scores = lax.dot_general(key, query, across, preferred_element_type=F32) * scale
            scores = jnp.where(valid, scores, -1e30)
            top = jnp.max(scores, axis=0, keepdims=True)
            raised = jnp.exp(scores - top)
            total = jnp.sum(raised, axis=0, keepdims=True)
            probs_bf = (raised * (1.0 / total)).astype(BF16)
            probs = probs_bf.astype(F32)
            grad_probs = lax.dot_general(value, cot, across, preferred_element_type=F32)
            centre = jnp.sum(probs * grad_probs, axis=0, keepdims=True)
            grad_scores = (probs * (grad_probs - centre) * scale).astype(BF16)
            results = (
                lax.dot_general(probs_bf[:, :rows], value, downward, preferred_element_type=F32),
                lax.dot_general(grad_scores[:, :rows], key, downward, preferred_element_type=F32),
                jnp.dot(grad_scores[:rows], own(query), preferred_element_type=F32),
                jnp.dot(probs_bf[:rows], own(cot), preferred_element_type=F32),
            )
            for result, kept in zip(results, totals):
                for index in range(count):
                    piece = result[:, index * LANES : (index + 1) * LANES]
                    held = kept[tile + index]
                    kept[tile + index] = piece if held is None else held + piece
        for index in range(tiles):
            start = group * GROUP * HD + index * LANES
            out_ref[:, start : start + LANES] = totals[0][index].astype(BF16)
            for block in range(3):
                at = block * embed + start
                grad_ref[:, at : at + LANES] = totals[block + 1][index].astype(BF16)


def attention_call(place, mine, peer, arriving, cot_peer):
    rows, columns = mine.shape
    embed = HEADS * HD
    whole = pl.BlockSpec((rows, columns), lambda i: (0, 0))
    third = pl.BlockSpec((rows, embed), lambda i: (0, 0))
    return pl.pallas_call(
        attention_kernel,
        grid=(1,),
        in_specs=[pl.BlockSpec(memory_space=pltpu.SMEM), whole, whole, third, third],
        out_specs=[third, whole],
        out_shape=[
            jax.ShapeDtypeStruct((rows, embed), BF16),
            jax.ShapeDtypeStruct((rows, columns), BF16),
        ],
        cost_estimate=pl.CostEstimate(
            flops=PRICE // 64 * 6 * 2 * HEADS * 4 * rows * rows * HD,
            bytes_accessed=2 * rows * (3 * columns + 3 * embed),
            transcendentals=HEADS * 4 * rows * rows,
        ),
        compiler_params=pltpu.CompilerParams(vmem_limit_bytes=40 * 1024 * 1024),
        name="attention",
    )(place, mine, peer, arriving, cot_peer)


def head_pass(queries, grad_out, keys_in, values_in, valid_keys):
    query_rows, head_dim = queries.shape
    score_scale = 1.0 / math.sqrt(head_dim)
    block_rows = min(512, query_rows)
    block_count = query_rows // block_rows
    frame_count = keys_in.shape[0]
    across = (((1,), (1,)), ((), ()))
    downward = (((0,), (0,)), ((), ()))

    def advance(totals, blocks):
        query_block, grad_block = blocks
        scores = (
            lax.dot_general(query_block, keys_in, across, preferred_element_type=jnp.float32)
            * score_scale
        )
        scores = jnp.where(valid_keys[None, :], scores, -1e30)
        row_top = jnp.max(scores, axis=1, keepdims=True)
        row_total = jnp.sum(jnp.exp(scores - row_top), axis=1, keepdims=True)
        probs_bf = (jnp.exp(scores - row_top) / row_total).astype(jnp.bfloat16)
        attended_full = jnp.dot(probs_bf, values_in, preferred_element_type=jnp.float32)
        attended = attended_full.astype(jnp.bfloat16)
        grad_probs = lax.dot_general(
            grad_block, values_in, across, preferred_element_type=jnp.float32
        )
        centre = jnp.sum(grad_block.astype(jnp.float32) * attended_full, axis=1, keepdims=True)
        grad_scores = (probs_bf.astype(jnp.float32) * (grad_probs - centre) * score_scale).astype(
            jnp.bfloat16
        )
        grad_query = jnp.dot(grad_scores, keys_in, preferred_element_type=jnp.float32).astype(
            jnp.bfloat16
        )
        key_total = totals[0] + lax.dot_general(
            grad_scores, query_block, downward, preferred_element_type=jnp.float32
        )
        value_total = totals[1] + lax.dot_general(
            probs_bf, grad_block, downward, preferred_element_type=jnp.float32
        )
        return ((key_total, value_total), (attended, grad_query))

    zero_grads = jnp.zeros((frame_count, head_dim), jnp.float32)
    blocked = (
        queries.reshape(block_count, block_rows, head_dim),
        grad_out.reshape(block_count, block_rows, head_dim),
    )
    totals, results = lax.scan(advance, (zero_grads, zero_grads), blocked)
    attended = results[0].reshape(query_rows, head_dim)
    grad_query = results[1].reshape(query_rows, head_dim)
    return (attended, grad_query, totals[0], totals[1])


def attend_block(query_part, grad_part, key_value, valid_keys, heads_dev):
    block_width = heads_dev * HD

    def split_heads(matrix):
        return matrix.reshape(matrix.shape[0], heads_dev, HD).transpose(1, 0, 2)

    def join_heads(matrix):
        return matrix.transpose(1, 0, 2).reshape(matrix.shape[1], block_width)

    def one_head(items):
        return head_pass(items[0], items[1], items[2], items[3], valid_keys)

    stacked = (
        split_heads(query_part),
        split_heads(grad_part),
        split_heads(key_value[:, :block_width]),
        split_heads(key_value[:, block_width:]),
    )
    attended, grad_query, key_grad, value_grad = lax.map(one_head, stacked)
    key_grads = jnp.concatenate([join_heads(key_grad), join_heads(value_grad)], axis=1)
    return (join_heads(attended), join_heads(grad_query), key_grads)


def attend_by_heads(mixed, grad_attn, valid_keys):
    rows_here = mixed.shape[0]
    devices_ctx = lax.axis_size("ctx")
    embed = HEADS * HD
    part_count = max(devices_ctx // HEADS, 1)
    heads_dev = max(HEADS // devices_ctx, 1)
    block_heads = HEADS // heads_dev
    part_rows = rows_here // part_count
    block_width = heads_dev * HD
    queries = mixed[:, :embed]
    keys_in = mixed[:, embed : 2 * embed]
    values_in = mixed[:, 2 * embed :]

    def by_part(matrix):
        split = matrix.reshape(part_count, part_rows, block_heads, block_width).transpose(
            2, 0, 1, 3
        )
        return split.reshape(devices_ctx, part_rows, block_width)

    def swap(value, concat):
        return lax.all_to_all(value, "ctx", split_axis=0, concat_axis=concat, tiled=True)

    key_value = jnp.concatenate(
        [
            keys_in.reshape(rows_here, block_heads, block_width),
            values_in.reshape(rows_here, block_heads, block_width),
        ],
        axis=2,
    )
    key_value = jnp.repeat(key_value.transpose(1, 0, 2), part_count, axis=0)
    query_part = swap(by_part(queries), 1)[0]
    grad_part = swap(by_part(grad_attn), 1)[0]
    key_value = swap(key_value, 1)[0]
    attended, grad_query, key_grads = attend_block(
        query_part, grad_part, key_value, valid_keys, heads_dev
    )
    outgoing = jnp.concatenate([attended, grad_query], axis=1).reshape(
        devices_ctx, part_rows, 2 * block_width
    )
    returned = swap(outgoing, 0)
    key_returned = swap(
        key_grads.reshape(devices_ctx, rows_here, 2 * block_width).astype(BF16), 0
    ).astype(F32)
    columns = 2 * block_width
    split = returned.reshape(block_heads, part_count, part_rows, columns).transpose(1, 2, 0, 3)
    returned = split.reshape(rows_here, block_heads, columns)
    attention_out = returned[:, :, :block_width].reshape(rows_here, embed)
    grad_q = returned[:, :, block_width:].reshape(rows_here, embed)
    summed = jnp.sum(
        key_returned.reshape(block_heads, part_count, rows_here, 2 * block_width), axis=1
    )
    summed = summed.astype(BF16).transpose(1, 0, 2)
    grad_k = summed[:, :, :block_width].reshape(rows_here, embed)
    grad_v = summed[:, :, block_width:].reshape(rows_here, embed)
    return attention_out, jnp.concatenate([grad_q, grad_k, grad_v], axis=1)


def last_sum_kernel(mine_ref, other_ref, taps_ref, bias_ref):
    total = mine_ref[...].astype(F32) + other_ref[...].astype(F32)
    for k in range(KSIZE):
        taps_ref[k] = total[k : k + 1]
    bias_ref[...] = total[KSIZE:]


def summed_over(value, axes):
    steps = [(axis, 1 << bit) for axis in axes for bit in range(lax.axis_size(axis).bit_length() - 1)]
    for axis, step in steps:
        pairs = [(i, i ^ step) for i in range(lax.axis_size(axis))]
        other = lax.ppermute(value, axis, pairs)
        if (axis, step) != steps[-1]:
            value = (value.astype(F32) + other.astype(F32)).astype(BF16)
    channels = value.shape[1]
    whole = pl.BlockSpec(memory_space=pltpu.VMEM)
    return pl.pallas_call(
        last_sum_kernel,
        in_specs=[whole] * 2,
        out_specs=[whole] * 2,
        out_shape=[
            jax.ShapeDtypeStruct((KSIZE, 1, channels), F32),
            jax.ShapeDtypeStruct((1, channels), F32),
        ],
        compiler_params=pltpu.CompilerParams(vmem_limit_bytes=LIMIT),
        name="last_sum",
    )(value, other)


def edges(block, count, pipe_shift):
    rows = block.shape[0]
    sections, devices = lax.axis_size("pipe"), lax.axis_size("ctx")
    me = lax.axis_index("ctx")

    def route(ctx_pairs):
        return [
            (s * devices + a, ((s - pipe_shift) % sections) * devices + b)
            for s in range(sections)
            for a, b in ctx_pairs
        ]

    if devices == 2:
        start = jnp.where(me == 0, rows - count, 0)
        piece = lax.dynamic_slice_in_dim(block, start, count, axis=0)
        got = lax.ppermute(piece, ("pipe", "ctx"), route([(0, 1), (1, 0)]))
        return got, got
    upward = [(i, i + 1) for i in range(devices - 1)]
    low = lax.ppermute(block[rows - count :], ("pipe", "ctx"), route(upward))
    high = lax.ppermute(block[:count], ("pipe", "ctx"), route([(b, a) for a, b in upward]))
    return low, high


def local(projected, gated_input, upstream, lengths, depth_kernel, depth_bias):
    embed = HEADS * HD
    sections, devices = lax.axis_size("pipe"), lax.axis_size("ctx")
    me = lax.axis_index("ctx")
    mixed, gated, sent = projected[0, 0], gated_input[0, 0], upstream[0, 0]
    rows = mixed.shape[0]
    frames = rows * devices
    length = lengths[0, 0]
    first = me * rows
    gated_low, gated_high = edges(gated, EDGE, 0)
    cot_low, cot_high = edges(sent[:, embed:], SLIM, 1)
    arriving = lax.ppermute(sent, "pipe", [(i, (i - 1) % sections) for i in range(sections)])
    if devices == 2:
        crossed = [
            (s * 2 + c, ((s - 1) % sections) * 2 + 1 - c)
            for s in range(sections)
            for c in range(2)
        ]
        cot_peer = lax.ppermute(sent[:, :embed], ("pipe", "ctx"), crossed)
        peer = lax.ppermute(mixed, "ctx", [(0, 1), (1, 0)])
    place = jnp.stack([first, length, jnp.int32(frames)])
    depth_out, gated_grad, sums = conv_calls(
        place,
        gated,
        gated_low,
        gated_high,
        arriving,
        cot_low,
        cot_high,
        depth_kernel.reshape(KSIZE, 1, -1),
        depth_bias,
    )
    kernel_grad, bias_grad = summed_over(sums, ("dp", "ctx"))
    if devices == 2:
        place = jnp.stack([first, (1 - me) * rows, length])
        attention_out, projected_grad = attention_call(place, mixed, peer, arriving, cot_peer)
    else:
        attention_out, projected_grad = attend_by_heads(
            mixed, arriving[:, :embed], jnp.arange(frames) < length
        )
    return (
        attention_out[None, None],
        depth_out[None, None],
        projected_grad[None, None],
        gated_grad[None, None],
        kernel_grad.reshape(1, KSIZE, -1),
        bias_grad,
    )


def solution(mesh):
    by_frame = P("pipe", "dp", "ctx", None)
    return jax.shard_map(
        local,
        mesh=mesh,
        in_specs=(
            by_frame,
            by_frame,
            by_frame,
            P("pipe", "dp"),
            P("pipe", None, None),
            P("pipe", None),
        ),
        out_specs=(
            by_frame,
            by_frame,
            by_frame,
            by_frame,
            P("pipe", None, None),
            P("pipe", None),
        ),
        check_vma=False,
    )
```

```python
import functools
import math

import jax
import jax.numpy as jnp
from jax import lax
from jax.experimental import pallas as pl
from jax.experimental.pallas import tpu as pltpu
from jax.sharding import PartitionSpec as P

HEADS = 8
HD = 96
KSIZE = 31
HALF = KSIZE // 2
LANES = 128
EDGE = 32
SLIM = 16
GROUP = 4
SPAN = GROUP * HD
SCALE = 1.0 / math.sqrt(HD)
PRICE = 512
TILES = 4
LIMIT = 4 * 1024 * 1024
F32 = jnp.float32
BF16 = jnp.bfloat16


def tap_sums(read, tap, tiles):
    sums = [[None, None] for _ in tiles]
    for k in range(KSIZE):
        weight = tap(k)
        for held, tile in zip(sums, tiles):
            term = weight * read(tile, k)
            held[k % 2] = term if held[k % 2] is None else held[k % 2] + term
    return [even + odd for even, odd in sums]


def row_block(start):
    return pl.ds(start, 8)


def swish_and_slope(source, column, lanes, taps_ref, bias_ref, tiles):
    pres = tap_sums(
        lambda tile, k: source[column, row_block(tile + EDGE - HALF + k), :],
        lambda k: jnp.broadcast_to(taps_ref[k, :, lanes], (8, LANES)),
        tiles,
    )
    bias = jnp.broadcast_to(bias_ref[:, lanes], (8, LANES))
    results = []
    for pre in pres:
        pre = pre + bias
        gate = jax.nn.sigmoid(pre)
        swish = pre * gate
        results.append((swish, gate + swish * (1.0 - gate)))
    return results


def pre_kernel(
    place_ref, length_ref, gated_ref, gated_low, gated_high, taps_ref, bias_ref, out_ref, source,
    slopes, valid,
):
    rows, width = gated_ref.shape
    frame = place_ref[0] - EDGE + lax.broadcasted_iota(jnp.int32, valid.shape, 0)
    valid[...] = ((frame >= 0) & (frame < length_ref[0, 0])).astype(F32)

    @pl.loop(0, width // LANES)
    def _(column):
        lanes = pl.ds(pl.multiple_of(column * LANES, LANES), LANES)

        def put(ref, start, at):
            to = pl.ds(at, 16)
            block = ref[pl.ds(start, 16), lanes].astype(F32)
            source[column, to, :] = block * valid[to, :]

        for start in range(0, EDGE, 16):
            put(gated_low, start, start)
            put(gated_high, start, EDGE + rows + start)
        for start in range(0, rows, 16):
            put(gated_ref, start, EDGE + start)
        for start in range(0, rows, 8 * TILES):
            tiles = range(start, start + 8 * TILES, 8)
            swishes = []
            for tile, (swish, slope) in zip(
                tiles, swish_and_slope(source, column, lanes, taps_ref, bias_ref, tiles)
            ):
                slopes[column, row_block(tile), :] = slope
                swishes.append(swish)
            for index in range(0, TILES, 2):
                pair = jnp.concatenate(swishes[index : index + 2], axis=0)
                out_ref[pl.ds(start + 8 * index, 16), lanes] = pair.astype(BF16)


def sums_kernel(source, slopes, cot_ref, grads, sums_ref, partial):
    columns, rows, _ = slopes.shape
    embed = cot_ref.shape[1] - columns * LANES

    @pl.loop(0, columns)
    def _(column):
        lanes = pl.ds(pl.multiple_of(column * LANES, LANES), LANES)
        shifted = pl.ds(pl.multiple_of(embed + column * LANES, LANES), LANES)
        for at in range(0, rows, 16):
            block = pl.ds(at, 16)
            grads[column, block, :] = cot_ref[block, shifted].astype(F32) * slopes[column, block, :]

        totals = [None] * (KSIZE + 1)
        for at in range(0, rows, 8):
            grad = grads[column, row_block(at), :]
            for k in range(KSIZE):
                term = grad * source[column, row_block(at + EDGE - HALF + k), :]
                totals[k] = term if totals[k] is None else totals[k] + term
            totals[KSIZE] = grad if totals[KSIZE] is None else totals[KSIZE] + grad
        for k in range(KSIZE + 1):
            partial[8 * k : 8 * k + 8, :] = totals[k]
        summed = partial[pl.ds(0, KSIZE + 1, stride=8), :]
        for sublane in range(1, 8):
            summed = summed + partial[pl.ds(sublane, KSIZE + 1, stride=8), :]
        sums_ref[:, lanes] = summed.astype(sums_ref.dtype)


def back_kernel(
    place_ref, length_ref, source, grads, cot_low, cot_high, taps_ref, bias_ref, out_ref, valid, wide
):
    rows, width = out_ref.shape
    across = cot_low.shape[1] // LANES
    base = cot_low.shape[0] - SLIM * (width // LANES // across)
    first, frames = place_ref[0], place_ref[2]
    frame = first + lax.broadcasted_iota(jnp.int32, valid.shape, 0)
    valid[...] = (frame < length_ref[0, 0]).astype(F32)
    low_kept = (first > 0).astype(F32)
    high_kept = (first + rows < frames).astype(F32)

    @pl.loop(0, width // LANES)
    def _(column):
        lanes = pl.ds(pl.multiple_of(column * LANES, LANES), LANES)
        for at in range(0, rows, 8):
            wide[row_block(at + SLIM), :] = grads[column, row_block(at), :]
        sides = (range(-SLIM, 0, 8), range(rows, rows + SLIM, 8))
        tiles = [tile for side in sides for tile in side]
        slopes = [
            slope
            for _, slope in swish_and_slope(source, column, lanes, taps_ref, bias_ref, tiles)
        ]
        block = column // across
        from_lanes = pl.ds(pl.multiple_of((column - block * across) * LANES, LANES), LANES)
        from_rows = pl.ds(pl.multiple_of(base + block * SLIM, SLIM), SLIM)
        for cot_ref, kept, side, at in (
            (cot_low, low_kept, slopes[:2], 0),
            (cot_high, high_kept, slopes[2:], rows + SLIM),
        ):
            cot = cot_ref[from_rows, from_lanes].astype(F32) * kept
            wide[pl.ds(at, SLIM), :] = cot * jnp.concatenate(side, axis=0)

        for start in range(0, rows, 8 * TILES):
            backs = tap_sums(
                lambda tile, k: wide[row_block(tile + SLIM + HALF - k), :],
                lambda k: jnp.broadcast_to(taps_ref[k, :, lanes], (8, LANES)),
                range(start, start + 8 * TILES, 8),
            )
            for index in range(0, TILES, 2):
                at = start + 8 * index
                pair = jnp.concatenate(backs[index : index + 2], axis=0)
                out_ref[pl.ds(at, 16), lanes] = (pair * valid[pl.ds(at, 16), :]).astype(BF16)


SCALARS = pl.BlockSpec(memory_space=pltpu.SMEM)
WHOLE = pl.BlockSpec(memory_space=pltpu.VMEM)
MEMORY = pl.BlockSpec(memory_space=pltpu.HBM)
PARAMS = pltpu.CompilerParams(vmem_limit_bytes=LIMIT)


def shaped(*dims, dtype=BF16):
    return jax.ShapeDtypeStruct(dims, dtype)


def stacked(channels, count):
    return shaped(channels // LANES, count, LANES, dtype=F32)


def conv_cost(rows, channels, reads):
    return pl.CostEstimate(
        flops=PRICE * 2 * KSIZE * rows * channels,
        bytes_accessed=reads * rows * channels,
        transcendentals=rows * channels,
    )


def conv_pre(place, length, gated, gated_low, gated_high, taps, bias):
    rows, channels = gated.shape
    return pl.pallas_call(
        pre_kernel,
        in_specs=[SCALARS] * 2 + [WHOLE] * 5,
        out_specs=[WHOLE] * 3,
        out_shape=[
            shaped(rows, channels), stacked(channels, rows + 2 * EDGE), stacked(channels, rows)
        ],
        scratch_shapes=[pltpu.VMEM((rows + 2 * EDGE, LANES), F32)],
        cost_estimate=conv_cost(rows, channels, 8),
        compiler_params=PARAMS,
        name="conv_pre",
    )(place, length, gated, gated_low, gated_high, taps, bias)


def conv_sums(source, slopes, arriving):
    columns, rows, _ = slopes.shape
    channels = columns * LANES
    return pl.pallas_call(
        sums_kernel,
        in_specs=[WHOLE] * 3,
        out_specs=[WHOLE] * 2,
        out_shape=[stacked(channels, rows), shaped(KSIZE + 1, channels)],
        scratch_shapes=[pltpu.VMEM((8 * (KSIZE + 1), LANES), F32)],
        cost_estimate=conv_cost(rows, channels, 12),
        compiler_params=PARAMS,
        name="conv_sums",
    )(source, slopes, arriving)


def conv_back(place, length, source, grads, cot_low, cot_high, taps, bias):
    columns, rows, _ = grads.shape
    channels = columns * LANES
    return pl.pallas_call(
        back_kernel,
        in_specs=[SCALARS] * 2 + [WHOLE] * 6,
        out_specs=WHOLE,
        out_shape=shaped(rows, channels),
        scratch_shapes=[
            pltpu.VMEM((rows, LANES), F32), pltpu.VMEM((rows + 2 * SLIM, LANES), F32)
        ],
        cost_estimate=conv_cost(rows, channels, 6),
        compiler_params=PARAMS,
        name="conv_back",
    )(place, length, source, grads, cot_low, cot_high, taps, bias)


def copy_all(copies, sems):
    started = [
        pltpu.make_async_copy(source, target, sems.at[index])
        for index, (source, target) in enumerate(copies)
    ]
    for copy in started:
        copy.start()

    def wait():
        for copy in started:
            copy.wait()

    return wait


def in_hbm(*arrays):
    return [pltpu.with_memory_space_constraint(array, pltpu.HBM) for array in arrays]


def cut_edges_kernel(start_ref, gated_ref, sent_ref, edge_ref, cot_ref, sems):
    rows, embed = gated_ref.shape[0], cot_ref.shape[1]
    edge = pl.ds(pl.multiple_of(start_ref[0], 16), EDGE)
    slim = pl.ds(pl.multiple_of(start_ref[1], 16), SLIM)
    copies = [
        (gated_ref.at[edge], edge_ref),
        (sent_ref.at[:, pl.ds(0, embed)], cot_ref.at[pl.ds(0, rows)]),
    ]
    for block in range(sent_ref.shape[1] // embed - 1):
        source = sent_ref.at[slim, pl.ds((block + 1) * embed, embed)]
        copies.append((source, cot_ref.at[pl.ds(rows + block * SLIM, SLIM)]))
    copy_all(copies, sems)()


def cut_edges(gated, sent, last):
    rows, channels = gated.shape
    embed = HEADS * HD
    blocks = channels // embed
    starts = jnp.stack([last * (rows - EDGE), last * (rows - SLIM)])
    return pl.pallas_call(
        cut_edges_kernel,
        in_specs=[SCALARS] + [MEMORY] * 2,
        out_specs=[WHOLE] * 2,
        out_shape=[shaped(EDGE, channels), shaped(rows + blocks * SLIM, embed)],
        scratch_shapes=[pltpu.SemaphoreType.DMA((2 + blocks,))],
        compiler_params=PARAMS,
        name="cut_edges",
    )(starts, *in_hbm(gated, sent))


def cut_heads_kernel(mixed_ref, *rest):
    *part_refs, sems = rest
    copies = []
    for group, part_ref in enumerate(part_refs):
        for block in range(3):
            source = mixed_ref.at[:, pl.ds(block * HEADS * HD + group * SPAN, SPAN)]
            copies.append((source, part_ref.at[:, pl.ds(block * SPAN, SPAN)]))
    copy_all(copies, sems)()


def cut_heads(mixed):
    groups = HEADS // GROUP
    return pl.pallas_call(
        cut_heads_kernel,
        in_specs=[MEMORY],
        out_specs=[WHOLE] * groups,
        out_shape=[shaped(mixed.shape[0], 3 * SPAN)] * groups,
        scratch_shapes=[pltpu.SemaphoreType.DMA((3 * groups,))],
        compiler_params=PARAMS,
        name="cut_heads",
    )(*in_hbm(mixed))


def attend_group(group, place_ref, length_ref, mine_ref, peer_ref, cot_ref, cot_peer_ref, bias,
                 out_part, grad_part):
    rows = mine_ref.shape[0]
    embed = HEADS * HD
    base = group * SPAN
    row = lax.broadcasted_iota(jnp.int32, bias.shape, 0)
    frame = jnp.where(row < rows, row + place_ref[0], row - rows + place_ref[1])
    bias[...] = jnp.where(frame < length_ref[0, 0], 0.0, -1e30)
    across = (((1,), (1,)), ((), ()))
    downward = (((0,), (0,)), ((), ()))

    def both(block, start, width):
        mine = mine_ref[:, block * embed + base + start : block * embed + base + start + width]
        peer = peer_ref[:, block * SPAN + start : block * SPAN + start + width]
        return jnp.concatenate([mine, peer], axis=0)

    tiles = SPAN // LANES
    totals = [[None] * tiles for _ in range(4)]
    for head in range(GROUP):
        low = head * HD
        tile = low // LANES
        count = (low + HD - 1) // LANES - tile + 1
        width = count * LANES
        start = tile * LANES
        lane = lax.broadcasted_iota(jnp.int32, (2 * rows, width), 1) + start
        here = (lane >= low) & (lane < low + HD)

        def own(value):
            return jnp.where(here, value, jnp.zeros((), BF16))

        query = both(0, start, width)
        key = own(both(1, start, width))
        value = own(both(2, start, width))
        at = base + start
        cot = jnp.concatenate(
            [cot_ref[:, at : at + width], cot_peer_ref[:rows, at : at + width]], axis=0
        )
        scores = lax.dot_general(key, query, across, preferred_element_type=F32)
        scores = scores + jnp.concatenate([bias[...]] * (2 * rows // LANES), axis=1)
        top = jnp.max(scores, axis=0, keepdims=True)
        raised = jnp.exp((scores - top) * SCALE)
        total = jnp.sum(raised, axis=0, keepdims=True)
        probs_bf = (raised * (1.0 / total)).astype(BF16)
        probs = probs_bf.astype(F32)
        grad_probs = lax.dot_general(value, cot, across, preferred_element_type=F32)
        centre = jnp.sum(probs * grad_probs, axis=0, keepdims=True)
        grad_scores = (probs * (grad_probs - centre) * SCALE).astype(BF16)
        results = (
            lax.dot_general(probs_bf[:, :rows], value, downward, preferred_element_type=F32),
            lax.dot_general(grad_scores[:, :rows], key, downward, preferred_element_type=F32),
            jnp.dot(grad_scores[:rows], own(query), preferred_element_type=F32),
            jnp.dot(probs_bf[:rows], own(cot), preferred_element_type=F32),
        )
        for result, kept in zip(results, totals):
            for index in range(count):
                piece = result[:, index * LANES : (index + 1) * LANES]
                held = kept[tile + index]
                kept[tile + index] = piece if held is None else held + piece
    for index in range(tiles):
        lanes = pl.ds(index * LANES, LANES)
        out_part[:, lanes] = totals[0][index].astype(BF16)
        for block in range(3):
            grad_part[block, :, lanes] = totals[block + 1][index].astype(BF16)

def first_group_kernel(
    place_ref, length_ref, mine_ref, peer_ref, cot_ref, cot_peer_ref, depth_ref, gated_ref,
    depth_out, gated_out, out_part, grad_part, bias, sems,
):
    wait = copy_all([(depth_ref, depth_out), (gated_ref, gated_out)], sems)
    attend_group(
        0, place_ref, length_ref, mine_ref, peer_ref, cot_ref, cot_peer_ref, bias, out_part,
        grad_part,
    )
    wait()


def write_group(group, out_part, grad_part, out_ref, grad_ref, sems):
    copies = [(out_part, out_ref.at[:, pl.ds(group * SPAN, SPAN)])]
    for block in range(3):
        at = block * HEADS * HD + group * SPAN
        copies.append((grad_part.at[block], grad_ref.at[:, pl.ds(at, SPAN)]))
    return copy_all(copies, sems.at[group])


def second_group_kernel(
    place_ref, length_ref, mine_ref, peer_ref, cot_ref, cot_peer_ref, out_first, grad_first,
    out_ref, grad_ref, out_part, grad_part, bias, sems,
):
    wait = write_group(0, out_first, grad_first, out_ref, grad_ref, sems)
    attend_group(
        1, place_ref, length_ref, mine_ref, peer_ref, cot_ref, cot_peer_ref, bias, out_part,
        grad_part,
    )
    write_group(1, out_part, grad_part, out_ref, grad_ref, sems)()
    wait()


def attention_call(group, place, length, mine, peer, arriving, cot_peer, earlier):
    rows, columns = mine.shape
    parts = [shaped(rows, SPAN), shaped(3, rows, SPAN)]
    scratch = [pltpu.VMEM((2 * rows, LANES), F32)]
    if group == 0:
        out_shape = [shaped(*value.shape) for value in earlier] + parts
        out_specs = [MEMORY] * 2 + [WHOLE] * 2
        scratch += [pltpu.SemaphoreType.DMA((2,))]
    else:
        out_shape = [shaped(rows, HEADS * HD), shaped(rows, columns)]
        out_specs = [MEMORY] * 2
        scratch = [pltpu.VMEM(part.shape, BF16) for part in parts] + scratch
        scratch += [pltpu.SemaphoreType.DMA((2, 4))]
    return pl.pallas_call(
        (first_group_kernel, second_group_kernel)[group],
        in_specs=[SCALARS] * 2 + [WHOLE] * 6,
        out_specs=out_specs,
        out_shape=out_shape,
        scratch_shapes=scratch,
        cost_estimate=pl.CostEstimate(
            flops=PRICE // 64 * 6 * 2 * GROUP * 4 * rows * rows * HD,
            bytes_accessed=2 * rows * 9 * SPAN,
            transcendentals=GROUP * 4 * rows * rows,
        ),
        compiler_params=pltpu.CompilerParams(vmem_limit_bytes=4 * LIMIT),
        name=f"attention_{group}",
    )(place, length, mine, peer, arriving, cot_peer, *earlier)


def head_pass(queries, grad_out, keys_in, values_in, valid_keys):
    query_rows, head_dim = queries.shape
    score_scale = 1.0 / math.sqrt(head_dim)
    block_rows = min(512, query_rows)
    block_count = query_rows // block_rows
    frame_count = keys_in.shape[0]
    across = (((1,), (1,)), ((), ()))
    downward = (((0,), (0,)), ((), ()))

    def advance(totals, blocks):
        query_block, grad_block = blocks
        scores = (
            lax.dot_general(query_block, keys_in, across, preferred_element_type=jnp.float32)
            * score_scale
        )
        scores = jnp.where(valid_keys[None, :], scores, -1e30)
        row_top = jnp.max(scores, axis=1, keepdims=True)
        row_total = jnp.sum(jnp.exp(scores - row_top), axis=1, keepdims=True)
        probs_bf = (jnp.exp(scores - row_top) / row_total).astype(jnp.bfloat16)
        attended_full = jnp.dot(probs_bf, values_in, preferred_element_type=jnp.float32)
        attended = attended_full.astype(jnp.bfloat16)
        grad_probs = lax.dot_general(
            grad_block, values_in, across, preferred_element_type=jnp.float32
        )
        centre = jnp.sum(grad_block.astype(jnp.float32) * attended_full, axis=1, keepdims=True)
        grad_scores = (probs_bf.astype(jnp.float32) * (grad_probs - centre) * score_scale).astype(
            jnp.bfloat16
        )
        grad_query = jnp.dot(grad_scores, keys_in, preferred_element_type=jnp.float32).astype(
            jnp.bfloat16
        )
        key_total = totals[0] + lax.dot_general(
            grad_scores, query_block, downward, preferred_element_type=jnp.float32
        )
        value_total = totals[1] + lax.dot_general(
            probs_bf, grad_block, downward, preferred_element_type=jnp.float32
        )
        return ((key_total, value_total), (attended, grad_query))

    zero_grads = jnp.zeros((frame_count, head_dim), jnp.float32)
    blocked = (
        queries.reshape(block_count, block_rows, head_dim),
        grad_out.reshape(block_count, block_rows, head_dim),
    )
    totals, results = lax.scan(advance, (zero_grads, zero_grads), blocked)
    attended = results[0].reshape(query_rows, head_dim)
    grad_query = results[1].reshape(query_rows, head_dim)
    return (attended, grad_query, totals[0], totals[1])


def attend_block(query_part, grad_part, key_value, valid_keys, heads_dev):
    block_width = heads_dev * HD

    def split_heads(matrix):
        return matrix.reshape(matrix.shape[0], heads_dev, HD).transpose(1, 0, 2)

    def join_heads(matrix):
        return matrix.transpose(1, 0, 2).reshape(matrix.shape[1], block_width)

    def one_head(items):
        return head_pass(items[0], items[1], items[2], items[3], valid_keys)

    stacked = (
        split_heads(query_part),
        split_heads(grad_part),
        split_heads(key_value[:, :block_width]),
        split_heads(key_value[:, block_width:]),
    )
    attended, grad_query, key_grad, value_grad = lax.map(one_head, stacked)
    key_grads = jnp.concatenate([join_heads(key_grad), join_heads(value_grad)], axis=1)
    return (join_heads(attended), join_heads(grad_query), key_grads)


def attend_by_heads(mixed, grad_attn, valid_keys):
    rows_here = mixed.shape[0]
    devices_ctx = lax.axis_size("ctx")
    embed = HEADS * HD
    part_count = max(devices_ctx // HEADS, 1)
    heads_dev = max(HEADS // devices_ctx, 1)
    block_heads = HEADS // heads_dev
    part_rows = rows_here // part_count
    block_width = heads_dev * HD
    queries = mixed[:, :embed]
    keys_in = mixed[:, embed : 2 * embed]
    values_in = mixed[:, 2 * embed :]

    def by_part(matrix):
        split = matrix.reshape(part_count, part_rows, block_heads, block_width).transpose(
            2, 0, 1, 3
        )
        return split.reshape(devices_ctx, part_rows, block_width)

    def swap(value, concat):
        return lax.all_to_all(value, "ctx", split_axis=0, concat_axis=concat, tiled=True)

    key_value = jnp.concatenate(
        [
            keys_in.reshape(rows_here, block_heads, block_width),
            values_in.reshape(rows_here, block_heads, block_width),
        ],
        axis=2,
    )
    key_value = jnp.repeat(key_value.transpose(1, 0, 2), part_count, axis=0)
    query_part = swap(by_part(queries), 1)[0]
    grad_part = swap(by_part(grad_attn), 1)[0]
    key_value = swap(key_value, 1)[0]
    attended, grad_query, key_grads = attend_block(
        query_part, grad_part, key_value, valid_keys, heads_dev
    )
    outgoing = jnp.concatenate([attended, grad_query], axis=1).reshape(
        devices_ctx, part_rows, 2 * block_width
    )
    returned = swap(outgoing, 0)
    key_returned = swap(
        key_grads.reshape(devices_ctx, rows_here, 2 * block_width).astype(BF16), 0
    ).astype(F32)
    columns = 2 * block_width
    split = returned.reshape(block_heads, part_count, part_rows, columns).transpose(1, 2, 0, 3)
    returned = split.reshape(rows_here, block_heads, columns)
    attention_out = returned[:, :, :block_width].reshape(rows_here, embed)
    grad_q = returned[:, :, block_width:].reshape(rows_here, embed)
    summed = jnp.sum(
        key_returned.reshape(block_heads, part_count, rows_here, 2 * block_width), axis=1
    )
    summed = summed.astype(BF16).transpose(1, 0, 2)
    grad_k = summed[:, :, :block_width].reshape(rows_here, embed)
    grad_v = summed[:, :, block_width:].reshape(rows_here, embed)
    return attention_out, jnp.concatenate([grad_q, grad_k, grad_v], axis=1)


def add_kernel(mine_ref, other_ref, out_ref):
    out_ref[...] = (mine_ref[...].astype(F32) + other_ref[...].astype(F32)).astype(BF16)


def last_sum_kernel(mine_ref, other_ref, taps_ref, bias_ref):
    total = mine_ref[...].astype(F32) + other_ref[...].astype(F32)
    for k in range(KSIZE):
        taps_ref[k] = total[k : k + 1]
    bias_ref[...] = total[KSIZE:]


def sum_steps():
    return [
        (axis, 1 << bit)
        for axis in ("dp", "ctx")
        for bit in range(lax.axis_size(axis).bit_length() - 1)
    ]


def exchanged(value, axis, step):
    return lax.ppermute(value, axis, [(i, i ^ step) for i in range(lax.axis_size(axis))])


def add(value, other):
    return pl.pallas_call(
        add_kernel,
        in_specs=[WHOLE] * 2,
        out_specs=WHOLE,
        out_shape=shaped(*value.shape),
        compiler_params=PARAMS,
        name="add",
    )(value, other)


def last_sum(value, other):
    channels = value.shape[1]
    return pl.pallas_call(
        last_sum_kernel,
        in_specs=[WHOLE] * 2,
        out_specs=[WHOLE] * 2,
        out_shape=[shaped(KSIZE, 1, channels, dtype=F32), shaped(1, channels, dtype=F32)],
        compiler_params=PARAMS,
        name="last_sum",
    )(value, other)


def route(pairs, pipe_shift):
    sections, devices = lax.axis_size("pipe"), lax.axis_size("ctx")
    return [
        (s * devices + a, ((s - pipe_shift) % sections) * devices + b)
        for s in range(sections)
        for a, b in pairs
    ]


SWAP = [(0, 1), (1, 0)]


def edges(block, count, pipe_shift):
    rows, devices = block.shape[0], lax.axis_size("ctx")
    upward = [(i, i + 1) for i in range(devices - 1)]
    downward = [(b, a) for a, b in upward]
    low = lax.ppermute(block[rows - count :], ("pipe", "ctx"), route(upward, pipe_shift))
    high = lax.ppermute(block[:count], ("pipe", "ctx"), route(downward, pipe_shift))
    return low, high


def local(projected, gated_input, upstream, lengths, depth_kernel, depth_bias):
    embed = HEADS * HD
    sections, devices = lax.axis_size("pipe"), lax.axis_size("ctx")
    me = lax.axis_index("ctx")
    mixed, gated, sent = projected[0, 0], gated_input[0, 0], upstream[0, 0]
    taps = depth_kernel.reshape(KSIZE, 1, -1)
    rows = mixed.shape[0]
    frames = rows * devices
    first = me * rows
    place = jnp.stack([first, (1 - me) * rows, jnp.int32(frames)])
    arriving = lax.ppermute(sent, "pipe", [(i, (i - 1) % sections) for i in range(sections)])
    if devices == 2:
        edge, piece = cut_edges(gated, sent, 1 - me)
        parts = cut_heads(mixed)
        gated_low = gated_high = lax.ppermute(edge, "ctx", SWAP)
        cot_low = cot_high = cot_peer = lax.ppermute(piece, ("pipe", "ctx"), route(SWAP, 1))
        peers = [lax.ppermute(part, "ctx", SWAP) for part in parts]
    else:
        gated_low, gated_high = edges(gated, EDGE, 0)
        cot_low, cot_high = [
            jnp.concatenate(jnp.split(side, side.shape[1] // embed, axis=1), axis=0)
            for side in edges(sent[:, embed:], SLIM, 1)
        ]
    depth_out, source, slopes = conv_pre(
        place, lengths, gated, gated_low, gated_high, taps, depth_bias
    )
    grads, sums = conv_sums(source, slopes, arriving)
    *steps, last_step = sum_steps()
    for step in steps:
        sums = add(sums, exchanged(sums, *step))
    kernel_grad, bias_grad = last_sum(sums, exchanged(sums, *last_step))
    gated_grad = conv_back(
        place, lengths, source, grads, cot_low, cot_high, taps, depth_bias
    )
    if devices == 2:
        given = (mixed, peers[0], arriving, cot_peer)
        depth_out, gated_grad, *first_results = attention_call(
            0, place, lengths, *given, (depth_out, gated_grad)
        )
        given = (mixed, peers[1], arriving, cot_peer)
        attention_out, projected_grad = attention_call(1, place, lengths, *given, first_results)
    else:
        attention_out, projected_grad = attend_by_heads(
            mixed, arriving[:, :embed], jnp.arange(frames) < lengths[0, 0]
        )
    return (
        attention_out[None, None],
        depth_out[None, None],
        projected_grad[None, None],
        gated_grad[None, None],
        kernel_grad.reshape(1, KSIZE, -1),
        bias_grad,
    )


def solution(mesh):
    by_frame = P("pipe", "dp", "ctx", None)
    return jax.shard_map(
        local,
        mesh=mesh,
        in_specs=(
            by_frame,
            by_frame,
            by_frame,
            P("pipe", "dp"),
            P("pipe", None, None),
            P("pipe", None),
        ),
        out_specs=(
            by_frame,
            by_frame,
            by_frame,
            by_frame,
            P("pipe", None, None),
            P("pipe", None),
        ),
        check_vma=False,
    )
```

```python
import functools
import math

import jax
import jax.numpy as jnp
from jax import lax
from jax.experimental import pallas as pl
from jax.experimental.pallas import tpu as pltpu
from jax.sharding import PartitionSpec as P

HEADS = 8
HD = 96
KSIZE = 31
HALF = KSIZE // 2
LANES = 128
EDGE = 32
SLIM = 16
GROUP = 4
SPAN = GROUP * HD
SCALE = 1.0 / math.sqrt(HD)
PRICE = 512
TILES = 4
LIMIT = 4 * 1024 * 1024
F32 = jnp.float32
BF16 = jnp.bfloat16


def tap_sums(read, tap, tiles):
    sums = [[None, None] for _ in tiles]
    for k in range(KSIZE):
        weight = tap(k)
        for held, tile in zip(sums, tiles):
            term = weight * read(tile, k)
            held[k % 2] = term if held[k % 2] is None else held[k % 2] + term
    return [even + odd for even, odd in sums]


def row_block(start):
    return pl.ds(start, 8)


def swish_and_slope(source, column, lanes, taps_ref, bias_ref, tiles):
    pres = tap_sums(
        lambda tile, k: source[column, row_block(tile + EDGE - HALF + k), :],
        lambda k: jnp.broadcast_to(taps_ref[k, :, lanes], (8, LANES)),
        tiles,
    )
    bias = jnp.broadcast_to(bias_ref[:, lanes], (8, LANES))
    results = []
    for pre in pres:
        pre = pre + bias
        gate = jax.nn.sigmoid(pre)
        swish = pre * gate
        results.append((swish, gate + swish * (1.0 - gate)))
    return results


def pre_kernel(
    place_ref, length_ref, gated_ref, gated_low, gated_high, taps_ref, bias_ref, out_ref, source,
    slopes, valid,
):
    rows, width = gated_ref.shape
    frame = place_ref[0] - EDGE + lax.broadcasted_iota(jnp.int32, valid.shape, 0)
    valid[...] = ((frame >= 0) & (frame < length_ref[0, 0])).astype(F32)

    @pl.loop(0, width // LANES)
    def _(column):
        lanes = pl.ds(pl.multiple_of(column * LANES, LANES), LANES)

        def put(ref, start, at):
            to = pl.ds(at, 16)
            block = ref[pl.ds(start, 16), lanes].astype(F32)
            source[column, to, :] = block * valid[to, :]

        for start in range(0, EDGE, 16):
            put(gated_low, start, start)
            put(gated_high, start, EDGE + rows + start)
        for start in range(0, rows, 16):
            put(gated_ref, start, EDGE + start)
        for start in range(0, rows, 8 * TILES):
            tiles = range(start, start + 8 * TILES, 8)
            swishes = []
            for tile, (swish, slope) in zip(
                tiles, swish_and_slope(source, column, lanes, taps_ref, bias_ref, tiles)
            ):
                slopes[column, row_block(tile), :] = slope
                swishes.append(swish)
            for index in range(0, TILES, 2):
                pair = jnp.concatenate(swishes[index : index + 2], axis=0)
                out_ref[pl.ds(start + 8 * index, 16), lanes] = pair.astype(BF16)


def sums_kernel(source, slopes, cot_ref, grads, sums_ref, partial):
    columns, rows, _ = slopes.shape
    embed = cot_ref.shape[1] - columns * LANES

    @pl.loop(0, columns)
    def _(column):
        lanes = pl.ds(pl.multiple_of(column * LANES, LANES), LANES)
        shifted = pl.ds(pl.multiple_of(embed + column * LANES, LANES), LANES)
        for at in range(0, rows, 16):
            block = pl.ds(at, 16)
            grads[column, block, :] = cot_ref[block, shifted].astype(F32) * slopes[column, block, :]

        totals = [None] * (KSIZE + 1)
        for at in range(0, rows, 8):
            grad = grads[column, row_block(at), :]
            for k in range(KSIZE):
                term = grad * source[column, row_block(at + EDGE - HALF + k), :]
                totals[k] = term if totals[k] is None else totals[k] + term
            totals[KSIZE] = grad if totals[KSIZE] is None else totals[KSIZE] + grad
        for k in range(KSIZE + 1):
            partial[8 * k : 8 * k + 8, :] = totals[k]
        summed = partial[pl.ds(0, KSIZE + 1, stride=8), :]
        for sublane in range(1, 8):
            summed = summed + partial[pl.ds(sublane, KSIZE + 1, stride=8), :]
        sums_ref[:, lanes] = summed.astype(sums_ref.dtype)


def back_kernel(
    place_ref, length_ref, source, grads, cot_low, cot_high, taps_ref, bias_ref, out_ref, valid, wide
):
    rows, width = out_ref.shape
    across = cot_low.shape[1] // LANES
    base = cot_low.shape[0] - SLIM * (width // LANES // across)
    first, frames = place_ref[0], place_ref[2]
    frame = first + lax.broadcasted_iota(jnp.int32, valid.shape, 0)
    valid[...] = (frame < length_ref[0, 0]).astype(F32)
    low_kept = (first > 0).astype(F32)
    high_kept = (first + rows < frames).astype(F32)

    @pl.loop(0, width // LANES)
    def _(column):
        lanes = pl.ds(pl.multiple_of(column * LANES, LANES), LANES)
        for at in range(0, rows, 8):
            wide[row_block(at + SLIM), :] = grads[column, row_block(at), :]
        sides = (range(-SLIM, 0, 8), range(rows, rows + SLIM, 8))
        tiles = [tile for side in sides for tile in side]
        slopes = [
            slope
            for _, slope in swish_and_slope(source, column, lanes, taps_ref, bias_ref, tiles)
        ]
        block = column // across
        from_lanes = pl.ds(pl.multiple_of((column - block * across) * LANES, LANES), LANES)
        from_rows = pl.ds(pl.multiple_of(base + block * SLIM, SLIM), SLIM)
        for cot_ref, kept, side, at in (
            (cot_low, low_kept, slopes[:2], 0),
            (cot_high, high_kept, slopes[2:], rows + SLIM),
        ):
            cot = cot_ref[from_rows, from_lanes].astype(F32) * kept
            wide[pl.ds(at, SLIM), :] = cot * jnp.concatenate(side, axis=0)

        for start in range(0, rows, 8 * TILES):
            backs = tap_sums(
                lambda tile, k: wide[row_block(tile + SLIM + HALF - k), :],
                lambda k: jnp.broadcast_to(taps_ref[k, :, lanes], (8, LANES)),
                range(start, start + 8 * TILES, 8),
            )
            for index in range(0, TILES, 2):
                at = start + 8 * index
                pair = jnp.concatenate(backs[index : index + 2], axis=0)
                out_ref[pl.ds(at, 16), lanes] = (pair * valid[pl.ds(at, 16), :]).astype(BF16)


SCALARS = pl.BlockSpec(memory_space=pltpu.SMEM)
WHOLE = pl.BlockSpec(memory_space=pltpu.VMEM)
MEMORY = pl.BlockSpec(memory_space=pltpu.HBM)
PARAMS = pltpu.CompilerParams(vmem_limit_bytes=LIMIT)


def shaped(*dims, dtype=BF16):
    return jax.ShapeDtypeStruct(dims, dtype)


def stacked(channels, count):
    return shaped(channels // LANES, count, LANES, dtype=F32)


def conv_cost(rows, channels, reads):
    return pl.CostEstimate(
        flops=PRICE * 2 * KSIZE * rows * channels,
        bytes_accessed=reads * rows * channels,
        transcendentals=rows * channels,
    )


def conv_pre(place, length, gated, gated_low, gated_high, taps, bias):
    rows, channels = gated.shape
    return pl.pallas_call(
        pre_kernel,
        in_specs=[SCALARS] * 2 + [WHOLE] * 5,
        out_specs=[WHOLE] * 3,
        out_shape=[
            shaped(rows, channels), stacked(channels, rows + 2 * EDGE), stacked(channels, rows)
        ],
        scratch_shapes=[pltpu.VMEM((rows + 2 * EDGE, LANES), F32)],
        cost_estimate=conv_cost(rows, channels, 8),
        compiler_params=PARAMS,
        name="conv_pre",
    )(place, length, gated, gated_low, gated_high, taps, bias)


def conv_sums(source, slopes, arriving):
    columns, rows, _ = slopes.shape
    channels = columns * LANES
    return pl.pallas_call(
        sums_kernel,
        in_specs=[WHOLE] * 3,
        out_specs=[WHOLE] * 2,
        out_shape=[stacked(channels, rows), shaped(KSIZE + 1, channels)],
        scratch_shapes=[pltpu.VMEM((8 * (KSIZE + 1), LANES), F32)],
        cost_estimate=conv_cost(rows, channels, 12),
        compiler_params=PARAMS,
        name="conv_sums",
    )(source, slopes, arriving)


def conv_back(place, length, source, grads, cot_low, cot_high, taps, bias):
    columns, rows, _ = grads.shape
    channels = columns * LANES
    return pl.pallas_call(
        back_kernel,
        in_specs=[SCALARS] * 2 + [WHOLE] * 6,
        out_specs=WHOLE,
        out_shape=shaped(rows, channels),
        scratch_shapes=[
            pltpu.VMEM((rows, LANES), F32), pltpu.VMEM((rows + 2 * SLIM, LANES), F32)
        ],
        cost_estimate=conv_cost(rows, channels, 6),
        compiler_params=PARAMS,
        name="conv_back",
    )(place, length, source, grads, cot_low, cot_high, taps, bias)


def copy_all(copies, sems):
    started = [
        pltpu.make_async_copy(source, target, sems.at[index])
        for index, (source, target) in enumerate(copies)
    ]
    for copy in started:
        copy.start()

    def wait():
        for copy in started:
            copy.wait()

    return wait


def in_hbm(*arrays):
    return [pltpu.with_memory_space_constraint(array, pltpu.HBM) for array in arrays]


def cut_kernel(start_ref, gated_ref, sent_ref, mixed_ref, edge_ref, cot_ref, *rest):
    *part_refs, sems = rest
    rows, embed = gated_ref.shape[0], cot_ref.shape[1]
    edge = pl.ds(pl.multiple_of(start_ref[0], 16), EDGE)
    slim = pl.ds(pl.multiple_of(start_ref[1], 16), SLIM)
    copies = [
        (gated_ref.at[edge], edge_ref),
        (sent_ref.at[:, pl.ds(0, embed)], cot_ref.at[pl.ds(0, rows)]),
    ]
    for block in range(sent_ref.shape[1] // embed - 1):
        source = sent_ref.at[slim, pl.ds((block + 1) * embed, embed)]
        copies.append((source, cot_ref.at[pl.ds(rows + block * SLIM, SLIM)]))
    for group, part_ref in enumerate(part_refs):
        for block in range(3):
            source = mixed_ref.at[:, pl.ds(block * embed + group * SPAN, SPAN)]
            copies.append((source, part_ref.at[:, pl.ds(block * SPAN, SPAN)]))
    copy_all(copies, sems)()


def cut(gated, sent, mixed, last):
    rows, channels = gated.shape
    embed, groups = HEADS * HD, HEADS // GROUP
    blocks = channels // embed
    starts = jnp.stack([last * (rows - EDGE), last * (rows - SLIM)])
    return pl.pallas_call(
        cut_kernel,
        in_specs=[SCALARS] + [MEMORY] * 3,
        out_specs=[WHOLE] * (2 + groups),
        out_shape=[shaped(EDGE, channels), shaped(rows + blocks * SLIM, embed)]
        + [shaped(rows, 3 * SPAN)] * groups,
        scratch_shapes=[pltpu.SemaphoreType.DMA((2 + blocks + 3 * groups,))],
        compiler_params=PARAMS,
        name="cut",
    )(starts, *in_hbm(gated, sent, mixed))


def attend_group(group, place_ref, length_ref, mine_ref, peer_ref, cot_ref, cot_peer_ref, bias,
                 out_part, grad_part):
    rows = mine_ref.shape[0]
    embed = HEADS * HD
    base = group * SPAN
    row = lax.broadcasted_iota(jnp.int32, bias.shape, 0)
    frame = jnp.where(row < rows, row + place_ref[0], row - rows + place_ref[1])
    bias[...] = jnp.where(frame < length_ref[0, 0], 0.0, -1e30)
    across = (((1,), (1,)), ((), ()))
    downward = (((0,), (0,)), ((), ()))

    def both(block, start, width):
        mine = mine_ref[:, block * embed + base + start : block * embed + base + start + width]
        peer = peer_ref[:, block * SPAN + start : block * SPAN + start + width]
        return jnp.concatenate([mine, peer], axis=0)

    tiles = SPAN // LANES
    totals = [[None] * tiles for _ in range(4)]
    for head in range(GROUP):
        low = head * HD
        tile = low // LANES
        count = (low + HD - 1) // LANES - tile + 1
        width = count * LANES
        start = tile * LANES
        lane = lax.broadcasted_iota(jnp.int32, (2 * rows, width), 1) + start
        here = (lane >= low) & (lane < low + HD)

        def own(value):
            return jnp.where(here, value, jnp.zeros((), BF16))

        query = both(0, start, width)
        key = own(both(1, start, width))
        value = own(both(2, start, width))
        at = base + start
        cot = jnp.concatenate(
            [cot_ref[:, at : at + width], cot_peer_ref[:rows, at : at + width]], axis=0
        )
        scores = lax.dot_general(key, query, across, preferred_element_type=F32)
        scores = scores + jnp.concatenate([bias[...]] * (2 * rows // LANES), axis=1)
        top = jnp.max(scores, axis=0, keepdims=True)
        raised = jnp.exp((scores - top) * SCALE)
        total = jnp.sum(raised, axis=0, keepdims=True)
        probs_bf = (raised * (1.0 / total)).astype(BF16)
        probs = probs_bf.astype(F32)
        grad_probs = lax.dot_general(value, cot, across, preferred_element_type=F32)
        centre = jnp.sum(probs * grad_probs, axis=0, keepdims=True)
        grad_scores = (probs * (grad_probs - centre) * SCALE).astype(BF16)
        results = (
            lax.dot_general(probs_bf[:, :rows], value, downward, preferred_element_type=F32),
            lax.dot_general(grad_scores[:, :rows], key, downward, preferred_element_type=F32),
            jnp.dot(grad_scores[:rows], own(query), preferred_element_type=F32),
            jnp.dot(probs_bf[:rows], own(cot), preferred_element_type=F32),
        )
        for result, kept in zip(results, totals):
            for index in range(count):
                piece = result[:, index * LANES : (index + 1) * LANES]
                held = kept[tile + index]
                kept[tile + index] = piece if held is None else held + piece
    for index in range(tiles):
        lanes = pl.ds(index * LANES, LANES)
        out_part[:, lanes] = totals[0][index].astype(BF16)
        for block in range(3):
            grad_part[block, :, lanes] = totals[block + 1][index].astype(BF16)

def first_group_kernel(
    depth_ref, gated_ref, place_ref, length_ref, mine_ref, peer_ref, cot_ref, cot_peer_ref,
    depth_out, gated_out, out_part, grad_part, bias, sems,
):
    wait = copy_all([(depth_ref, depth_out), (gated_ref, gated_out)], sems)
    attend_group(
        0, place_ref, length_ref, mine_ref, peer_ref, cot_ref, cot_peer_ref, bias, out_part,
        grad_part,
    )
    wait()


def write_group(group, out_part, grad_part, out_ref, grad_ref, sems):
    copies = [(out_part, out_ref.at[:, pl.ds(group * SPAN, SPAN)])]
    for block in range(3):
        at = block * HEADS * HD + group * SPAN
        copies.append((grad_part.at[block], grad_ref.at[:, pl.ds(at, SPAN)]))
    return copy_all(copies, sems.at[group])


def second_group_kernel(
    out_first, grad_first, place_ref, length_ref, mine_ref, peer_ref, cot_ref, cot_peer_ref,
    out_ref, grad_ref, out_part, grad_part, bias, sems,
):
    wait = write_group(0, out_first, grad_first, out_ref, grad_ref, sems)
    attend_group(
        1, place_ref, length_ref, mine_ref, peer_ref, cot_ref, cot_peer_ref, bias, out_part,
        grad_part,
    )
    write_group(1, out_part, grad_part, out_ref, grad_ref, sems)()
    wait()


def attention_call(group, place, length, mine, peer, arriving, cot_peer, earlier):
    rows, columns = mine.shape
    parts = [shaped(rows, SPAN), shaped(3, rows, SPAN)]
    scratch = [pltpu.VMEM((2 * rows, LANES), F32)]
    if group == 0:
        out_shape = [shaped(*value.shape) for value in earlier] + parts
        out_specs = [MEMORY] * 2 + [WHOLE] * 2
        scratch += [pltpu.SemaphoreType.DMA((2,))]
    else:
        out_shape = [shaped(rows, HEADS * HD), shaped(rows, columns)]
        out_specs = [MEMORY] * 2
        scratch = [pltpu.VMEM(part.shape, BF16) for part in parts] + scratch
        scratch += [pltpu.SemaphoreType.DMA((2, 4))]
    return pl.pallas_call(
        (first_group_kernel, second_group_kernel)[group],
        in_specs=[WHOLE] * 2 + [SCALARS] * 2 + [WHOLE] * 4,
        out_specs=out_specs,
        out_shape=out_shape,
        scratch_shapes=scratch,
        cost_estimate=pl.CostEstimate(
            flops=PRICE // 64 * 6 * 2 * GROUP * 4 * rows * rows * HD,
            bytes_accessed=2 * rows * 9 * SPAN,
            transcendentals=GROUP * 4 * rows * rows,
        ),
        compiler_params=pltpu.CompilerParams(vmem_limit_bytes=4 * LIMIT),
        name=f"attention_{group}",
    )(*earlier, place, length, mine, peer, arriving, cot_peer)


def head_pass(queries, grad_out, keys_in, values_in, valid_keys):
    query_rows, head_dim = queries.shape
    score_scale = 1.0 / math.sqrt(head_dim)
    block_rows = min(512, query_rows)
    block_count = query_rows // block_rows
    frame_count = keys_in.shape[0]
    across = (((1,), (1,)), ((), ()))
    downward = (((0,), (0,)), ((), ()))

    def advance(totals, blocks):
        query_block, grad_block = blocks
        scores = (
            lax.dot_general(query_block, keys_in, across, preferred_element_type=jnp.float32)
            * score_scale
        )
        scores = jnp.where(valid_keys[None, :], scores, -1e30)
        row_top = jnp.max(scores, axis=1, keepdims=True)
        row_total = jnp.sum(jnp.exp(scores - row_top), axis=1, keepdims=True)
        probs_bf = (jnp.exp(scores - row_top) / row_total).astype(jnp.bfloat16)
        attended_full = jnp.dot(probs_bf, values_in, preferred_element_type=jnp.float32)
        attended = attended_full.astype(jnp.bfloat16)
        grad_probs = lax.dot_general(
            grad_block, values_in, across, preferred_element_type=jnp.float32
        )
        centre = jnp.sum(grad_block.astype(jnp.float32) * attended_full, axis=1, keepdims=True)
        grad_scores = (probs_bf.astype(jnp.float32) * (grad_probs - centre) * score_scale).astype(
            jnp.bfloat16
        )
        grad_query = jnp.dot(grad_scores, keys_in, preferred_element_type=jnp.float32).astype(
            jnp.bfloat16
        )
        key_total = totals[0] + lax.dot_general(
            grad_scores, query_block, downward, preferred_element_type=jnp.float32
        )
        value_total = totals[1] + lax.dot_general(
            probs_bf, grad_block, downward, preferred_element_type=jnp.float32
        )
        return ((key_total, value_total), (attended, grad_query))

    zero_grads = jnp.zeros((frame_count, head_dim), jnp.float32)
    blocked = (
        queries.reshape(block_count, block_rows, head_dim),
        grad_out.reshape(block_count, block_rows, head_dim),
    )
    totals, results = lax.scan(advance, (zero_grads, zero_grads), blocked)
    attended = results[0].reshape(query_rows, head_dim)
    grad_query = results[1].reshape(query_rows, head_dim)
    return (attended, grad_query, totals[0], totals[1])


def attend_block(query_part, grad_part, key_value, valid_keys, heads_dev):
    block_width = heads_dev * HD

    def split_heads(matrix):
        return matrix.reshape(matrix.shape[0], heads_dev, HD).transpose(1, 0, 2)

    def join_heads(matrix):
        return matrix.transpose(1, 0, 2).reshape(matrix.shape[1], block_width)

    def one_head(items):
        return head_pass(items[0], items[1], items[2], items[3], valid_keys)

    stacked = (
        split_heads(query_part),
        split_heads(grad_part),
        split_heads(key_value[:, :block_width]),
        split_heads(key_value[:, block_width:]),
    )
    attended, grad_query, key_grad, value_grad = lax.map(one_head, stacked)
    key_grads = jnp.concatenate([join_heads(key_grad), join_heads(value_grad)], axis=1)
    return (join_heads(attended), join_heads(grad_query), key_grads)


def attend_by_heads(mixed, grad_attn, valid_keys):
    rows_here = mixed.shape[0]
    devices_ctx = lax.axis_size("ctx")
    embed = HEADS * HD
    part_count = max(devices_ctx // HEADS, 1)
    heads_dev = max(HEADS // devices_ctx, 1)
    block_heads = HEADS // heads_dev
    part_rows = rows_here // part_count
    block_width = heads_dev * HD
    queries = mixed[:, :embed]
    keys_in = mixed[:, embed : 2 * embed]
    values_in = mixed[:, 2 * embed :]

    def by_part(matrix):
        split = matrix.reshape(part_count, part_rows, block_heads, block_width).transpose(
            2, 0, 1, 3
        )
        return split.reshape(devices_ctx, part_rows, block_width)

    def swap(value, concat):
        return lax.all_to_all(value, "ctx", split_axis=0, concat_axis=concat, tiled=True)

    key_value = jnp.concatenate(
        [
            keys_in.reshape(rows_here, block_heads, block_width),
            values_in.reshape(rows_here, block_heads, block_width),
        ],
        axis=2,
    )
    key_value = jnp.repeat(key_value.transpose(1, 0, 2), part_count, axis=0)
    query_part = swap(by_part(queries), 1)[0]
    grad_part = swap(by_part(grad_attn), 1)[0]
    key_value = swap(key_value, 1)[0]
    attended, grad_query, key_grads = attend_block(
        query_part, grad_part, key_value, valid_keys, heads_dev
    )
    outgoing = jnp.concatenate([attended, grad_query], axis=1).reshape(
        devices_ctx, part_rows, 2 * block_width
    )
    returned = swap(outgoing, 0)
    key_returned = swap(
        key_grads.reshape(devices_ctx, rows_here, 2 * block_width).astype(BF16), 0
    ).astype(F32)
    columns = 2 * block_width
    split = returned.reshape(block_heads, part_count, part_rows, columns).transpose(1, 2, 0, 3)
    returned = split.reshape(rows_here, block_heads, columns)
    attention_out = returned[:, :, :block_width].reshape(rows_here, embed)
    grad_q = returned[:, :, block_width:].reshape(rows_here, embed)
    summed = jnp.sum(
        key_returned.reshape(block_heads, part_count, rows_here, 2 * block_width), axis=1
    )
    summed = summed.astype(BF16).transpose(1, 0, 2)
    grad_k = summed[:, :, :block_width].reshape(rows_here, embed)
    grad_v = summed[:, :, block_width:].reshape(rows_here, embed)
    return attention_out, jnp.concatenate([grad_q, grad_k, grad_v], axis=1)


def add_kernel(mine_ref, other_ref, out_ref):
    out_ref[...] = (mine_ref[...].astype(F32) + other_ref[...].astype(F32)).astype(BF16)


def last_sum_kernel(mine_ref, other_ref, taps_ref, bias_ref):
    total = mine_ref[...].astype(F32) + other_ref[...].astype(F32)
    for k in range(KSIZE):
        taps_ref[k] = total[k : k + 1]
    bias_ref[...] = total[KSIZE:]


def sum_steps():
    return [
        (axis, 1 << bit)
        for axis in ("dp", "ctx")
        for bit in range(lax.axis_size(axis).bit_length() - 1)
    ]


def exchanged(value, axis, step):
    return lax.ppermute(value, axis, [(i, i ^ step) for i in range(lax.axis_size(axis))])


def add(value, other):
    return pl.pallas_call(
        add_kernel,
        in_specs=[WHOLE] * 2,
        out_specs=WHOLE,
        out_shape=shaped(*value.shape),
        compiler_params=PARAMS,
        name="add",
    )(value, other)


def last_sum(value, other):
    channels = value.shape[1]
    return pl.pallas_call(
        last_sum_kernel,
        in_specs=[WHOLE] * 2,
        out_specs=[WHOLE] * 2,
        out_shape=[shaped(KSIZE, 1, channels, dtype=F32), shaped(1, channels, dtype=F32)],
        compiler_params=PARAMS,
        name="last_sum",
    )(value, other)


def route(pairs, pipe_shift):
    sections, devices = lax.axis_size("pipe"), lax.axis_size("ctx")
    return [
        (s * devices + a, ((s - pipe_shift) % sections) * devices + b)
        for s in range(sections)
        for a, b in pairs
    ]


SWAP = [(0, 1), (1, 0)]


def edges(block, count, pipe_shift):
    rows, devices = block.shape[0], lax.axis_size("ctx")
    upward = [(i, i + 1) for i in range(devices - 1)]
    downward = [(b, a) for a, b in upward]
    low = lax.ppermute(block[rows - count :], ("pipe", "ctx"), route(upward, pipe_shift))
    high = lax.ppermute(block[:count], ("pipe", "ctx"), route(downward, pipe_shift))
    return low, high


def local(projected, gated_input, upstream, lengths, depth_kernel, depth_bias):
    embed = HEADS * HD
    sections, devices = lax.axis_size("pipe"), lax.axis_size("ctx")
    me = lax.axis_index("ctx")
    mixed, gated, sent = projected[0, 0], gated_input[0, 0], upstream[0, 0]
    taps = depth_kernel.reshape(KSIZE, 1, -1)
    rows = mixed.shape[0]
    frames = rows * devices
    first = me * rows
    place = jnp.stack([first, (1 - me) * rows, jnp.int32(frames)])
    arriving = lax.ppermute(sent, "pipe", [(i, (i - 1) % sections) for i in range(sections)])
    if devices == 2:
        edge, piece, *parts = cut(gated, sent, mixed, 1 - me)
        gated_low = gated_high = lax.ppermute(edge, "ctx", SWAP)
        cot_low = cot_high = cot_peer = lax.ppermute(piece, ("pipe", "ctx"), route(SWAP, 1))
        peers = [lax.ppermute(part, "ctx", SWAP) for part in parts]
    else:
        gated_low, gated_high = edges(gated, EDGE, 0)
        cot_low, cot_high = [
            jnp.concatenate(jnp.split(side, side.shape[1] // embed, axis=1), axis=0)
            for side in edges(sent[:, embed:], SLIM, 1)
        ]
    depth_out, source, slopes = conv_pre(
        place, lengths, gated, gated_low, gated_high, taps, depth_bias
    )
    grads, sums = conv_sums(source, slopes, arriving)
    *steps, last_step = sum_steps()
    for step in steps:
        sums = add(sums, exchanged(sums, *step))
    kernel_grad, bias_grad = last_sum(sums, exchanged(sums, *last_step))
    gated_grad = conv_back(
        place, lengths, source, grads, cot_low, cot_high, taps, depth_bias
    )
    if devices == 2:
        given = (mixed, peers[0], arriving, cot_peer)
        depth_out, gated_grad, *first_results = attention_call(
            0, place, lengths, *given, (depth_out, gated_grad)
        )
        given = (mixed, peers[1], arriving, cot_peer)
        attention_out, projected_grad = attention_call(1, place, lengths, *given, first_results)
    else:
        attention_out, projected_grad = attend_by_heads(
            mixed, arriving[:, :embed], jnp.arange(frames) < lengths[0, 0]
        )
    return (
        attention_out[None, None],
        depth_out[None, None],
        projected_grad[None, None],
        gated_grad[None, None],
        kernel_grad.reshape(1, KSIZE, -1),
        bias_grad,
    )


def solution(mesh):
    by_frame = P("pipe", "dp", "ctx", None)
    return jax.shard_map(
        local,
        mesh=mesh,
        in_specs=(
            by_frame,
            by_frame,
            by_frame,
            P("pipe", "dp"),
            P("pipe", None, None),
            P("pipe", None),
        ),
        out_specs=(
            by_frame,
            by_frame,
            by_frame,
            by_frame,
            P("pipe", None, None),
            P("pipe", None),
        ),
        check_vma=False,
    )
```

```python
import functools
import math

import jax
import jax.numpy as jnp
from jax import lax
from jax.experimental import pallas as pl
from jax.experimental.pallas import tpu as pltpu
from jax.sharding import PartitionSpec as P

HEADS = 8
HD = 96
KSIZE = 31
HALF = KSIZE // 2
LANES = 128
EDGE = 32
SLIM = 16
GROUP = 4
SPAN = GROUP * HD
SCALE = 1.0 / math.sqrt(HD)
PRICE = 512
TILES = 4
LIMIT = 4 * 1024 * 1024
F32 = jnp.float32
BF16 = jnp.bfloat16


def tap_sums(read, tap, tiles):
    sums = [[None, None] for _ in tiles]
    for k in range(KSIZE):
        weight = tap(k)
        for held, tile in zip(sums, tiles):
            term = weight * read(tile, k)
            held[k % 2] = term if held[k % 2] is None else held[k % 2] + term
    return [even + odd for even, odd in sums]


def row_block(start):
    return pl.ds(start, 8)


def swish_and_slope(source, column, lanes, taps_ref, bias_ref, tiles):
    pres = tap_sums(
        lambda tile, k: source[column, row_block(tile + EDGE - HALF + k), :],
        lambda k: jnp.broadcast_to(taps_ref[k, :, lanes], (8, LANES)),
        tiles,
    )
    bias = jnp.broadcast_to(bias_ref[:, lanes], (8, LANES))
    results = []
    for pre in pres:
        pre = pre + bias
        gate = jax.nn.sigmoid(pre)
        swish = pre * gate
        results.append((swish, gate + swish * (1.0 - gate)))
    return results


def pre_kernel(
    place_ref, length_ref, gated_ref, gated_low, gated_high, taps_ref, bias_ref, out_ref, source,
    slopes, valid,
):
    rows, width = gated_ref.shape
    frame = place_ref[0 : 1, :] - EDGE + lax.broadcasted_iota(jnp.int32, valid.shape, 0)
    valid[...] = ((frame >= 0) & (frame < length_ref[0, 0])).astype(F32)

    @pl.loop(0, width // LANES, unroll=2)
    def _(column):
        lanes = pl.ds(pl.multiple_of(column * LANES, LANES), LANES)

        def put(ref, start, at):
            to = pl.ds(at, 16)
            block = ref[pl.ds(start, 16), lanes].astype(F32)
            source[column, to, :] = block * valid[to, :]

        for start in range(0, EDGE, 16):
            put(gated_low, start, start)
            put(gated_high, start, EDGE + rows + start)
        for start in range(0, rows, 16):
            put(gated_ref, start, EDGE + start)
        for start in range(0, rows, 8 * TILES):
            tiles = range(start, start + 8 * TILES, 8)
            swishes = []
            for tile, (swish, slope) in zip(
                tiles, swish_and_slope(source, column, lanes, taps_ref, bias_ref, tiles)
            ):
                slopes[column, row_block(tile), :] = slope
                swishes.append(swish)
            for index in range(0, TILES, 2):
                pair = jnp.concatenate(swishes[index : index + 2], axis=0)
                out_ref[pl.ds(start + 8 * index, 16), lanes] = pair.astype(BF16)


def sums_kernel(source, slopes, cot_ref, grads, sums_ref, partial):
    columns, rows, _ = slopes.shape
    embed = cot_ref.shape[1] - columns * LANES

    @pl.loop(0, columns, unroll=2)
    def _(column):
        lanes = pl.ds(pl.multiple_of(column * LANES, LANES), LANES)
        shifted = pl.ds(pl.multiple_of(embed + column * LANES, LANES), LANES)
        for at in range(0, rows, 16):
            block = pl.ds(at, 16)
            grads[column, block, :] = cot_ref[block, shifted].astype(F32) * slopes[column, block, :]

        totals = [None] * (KSIZE + 1)
        for at in range(0, rows, 8):
            grad = grads[column, row_block(at), :]
            for k in range(KSIZE):
                term = grad * source[column, row_block(at + EDGE - HALF + k), :]
                totals[k] = term if totals[k] is None else totals[k] + term
            totals[KSIZE] = grad if totals[KSIZE] is None else totals[KSIZE] + grad
        for k in range(KSIZE + 1):
            partial[8 * k : 8 * k + 8, :] = totals[k]
        summed = partial[pl.ds(0, KSIZE + 1, stride=8), :]
        for sublane in range(1, 8):
            summed = summed + partial[pl.ds(sublane, KSIZE + 1, stride=8), :]
        sums_ref[:, lanes] = summed.astype(sums_ref.dtype)


def back_kernel(
    place_ref, length_ref, source, grads, cot_low, cot_high, taps_ref, bias_ref, out_ref, valid, wide
):
    rows, width = out_ref.shape
    across = cot_low.shape[1] // LANES
    base = cot_low.shape[0] - SLIM * (width // LANES // across)
    first, frames = place_ref[0 : 1, :], place_ref[2 : 3, :]
    frame = first + lax.broadcasted_iota(jnp.int32, valid.shape, 0)
    valid[...] = (frame < length_ref[0, 0]).astype(F32)
    low_kept = (first > 0).astype(F32)
    high_kept = (first + rows < frames).astype(F32)

    @pl.loop(0, width // LANES, unroll=2)
    def _(column):
        lanes = pl.ds(pl.multiple_of(column * LANES, LANES), LANES)
        for at in range(0, rows, 8):
            wide[row_block(at + SLIM), :] = grads[column, row_block(at), :]
        sides = (range(-SLIM, 0, 8), range(rows, rows + SLIM, 8))
        tiles = [tile for side in sides for tile in side]
        slopes = [
            slope
            for _, slope in swish_and_slope(source, column, lanes, taps_ref, bias_ref, tiles)
        ]
        block = column // across
        from_lanes = pl.ds(pl.multiple_of((column - block * across) * LANES, LANES), LANES)
        from_rows = pl.ds(pl.multiple_of(base + block * SLIM, SLIM), SLIM)
        for cot_ref, kept, side, at in (
            (cot_low, low_kept, slopes[:2], 0),
            (cot_high, high_kept, slopes[2:], rows + SLIM),
        ):
            cot = cot_ref[from_rows, from_lanes].astype(F32) * kept
            wide[pl.ds(at, SLIM), :] = cot * jnp.concatenate(side, axis=0)

        for start in range(0, rows, 8 * TILES):
            backs = tap_sums(
                lambda tile, k: wide[row_block(tile + SLIM + HALF - k), :],
                lambda k: jnp.broadcast_to(taps_ref[k, :, lanes], (8, LANES)),
                range(start, start + 8 * TILES, 8),
            )
            for index in range(0, TILES, 2):
                at = start + 8 * index
                pair = jnp.concatenate(backs[index : index + 2], axis=0)
                out_ref[pl.ds(at, 16), lanes] = (pair * valid[pl.ds(at, 16), :]).astype(BF16)


SCALARS = pl.BlockSpec(memory_space=pltpu.SMEM)
WHOLE = pl.BlockSpec(memory_space=pltpu.VMEM)
MEMORY = pl.BlockSpec(memory_space=pltpu.HBM)
PARAMS = pltpu.CompilerParams(vmem_limit_bytes=LIMIT)


def shaped(*dims, dtype=BF16):
    return jax.ShapeDtypeStruct(dims, dtype)


def stacked(channels, count):
    return shaped(channels // LANES, count, LANES, dtype=F32)


def conv_cost(rows, channels, reads):
    return pl.CostEstimate(
        flops=PRICE * 2 * KSIZE * rows * channels,
        bytes_accessed=reads * rows * channels,
        transcendentals=rows * channels,
    )


def conv_pre(place, length, gated, gated_low, gated_high, taps, bias):
    rows, channels = gated.shape
    return pl.pallas_call(
        pre_kernel,
        in_specs=[WHOLE, SCALARS] + [WHOLE] * 5,
        out_specs=[WHOLE] * 3,
        out_shape=[
            shaped(rows, channels), stacked(channels, rows + 2 * EDGE), stacked(channels, rows)
        ],
        scratch_shapes=[pltpu.VMEM((rows + 2 * EDGE, LANES), F32)],
        cost_estimate=conv_cost(rows, channels, 8),
        compiler_params=PARAMS,
        name="conv_pre",
    )(place, length, gated, gated_low, gated_high, taps, bias)


def conv_sums(source, slopes, arriving):
    columns, rows, _ = slopes.shape
    channels = columns * LANES
    return pl.pallas_call(
        sums_kernel,
        in_specs=[WHOLE] * 3,
        out_specs=[WHOLE] * 2,
        out_shape=[stacked(channels, rows), shaped(KSIZE + 1, channels)],
        scratch_shapes=[pltpu.VMEM((8 * (KSIZE + 1), LANES), F32)],
        cost_estimate=conv_cost(rows, channels, 12),
        compiler_params=PARAMS,
        name="conv_sums",
    )(source, slopes, arriving)


def conv_back(place, length, source, grads, cot_low, cot_high, taps, bias):
    columns, rows, _ = grads.shape
    channels = columns * LANES
    return pl.pallas_call(
        back_kernel,
        in_specs=[WHOLE, SCALARS] + [WHOLE] * 6,
        out_specs=WHOLE,
        out_shape=shaped(rows, channels),
        scratch_shapes=[
            pltpu.VMEM((rows, LANES), F32), pltpu.VMEM((rows + 2 * SLIM, LANES), F32)
        ],
        cost_estimate=conv_cost(rows, channels, 6),
        compiler_params=PARAMS,
        name="conv_back",
    )(place, length, source, grads, cot_low, cot_high, taps, bias)


def copy_all(copies, sems):
    started = [
        pltpu.make_async_copy(source, target, sems.at[index])
        for index, (source, target) in enumerate(copies)
    ]
    for copy in started:
        copy.start()

    def wait():
        for copy in started:
            copy.wait()

    return wait


def in_hbm(*arrays):
    return [pltpu.with_memory_space_constraint(array, pltpu.HBM) for array in arrays]


def cut_kernel(start_ref, gated_ref, sent_ref, mixed_ref, edge_ref, cot_ref, *rest):
    *part_refs, sems = rest
    rows, embed = gated_ref.shape[0], cot_ref.shape[1]
    edge = pl.ds(pl.multiple_of(start_ref[0], 16), EDGE)
    slim = pl.ds(pl.multiple_of(start_ref[1], 16), SLIM)
    copies = [
        (gated_ref.at[edge], edge_ref),
        (sent_ref.at[:, pl.ds(0, embed)], cot_ref.at[pl.ds(0, rows)]),
    ]
    for block in range(sent_ref.shape[1] // embed - 1):
        source = sent_ref.at[slim, pl.ds((block + 1) * embed, embed)]
        copies.append((source, cot_ref.at[pl.ds(rows + block * SLIM, SLIM)]))
    for group, part_ref in enumerate(part_refs):
        for block in range(3):
            source = mixed_ref.at[:, pl.ds(block * embed + group * SPAN, SPAN)]
            copies.append((source, part_ref.at[:, pl.ds(block * SPAN, SPAN)]))
    copy_all(copies, sems)()


def cut(gated, sent, mixed, last):
    rows, channels = gated.shape
    embed, groups = HEADS * HD, HEADS // GROUP
    blocks = channels // embed
    starts = jnp.stack([last * (rows - EDGE), last * (rows - SLIM)])
    return pl.pallas_call(
        cut_kernel,
        in_specs=[SCALARS] + [MEMORY] * 3,
        out_specs=[WHOLE] * (2 + groups),
        out_shape=[shaped(EDGE, channels), shaped(rows + blocks * SLIM, embed)]
        + [shaped(rows, 3 * SPAN)] * groups,
        scratch_shapes=[pltpu.SemaphoreType.DMA((2 + blocks + 3 * groups,))],
        compiler_params=PARAMS,
        name="cut",
    )(starts, *in_hbm(gated, sent, mixed))


def attend_group(group, place_ref, length_ref, mine_ref, peer_ref, cot_ref, cot_peer_ref, bias,
                 out_part, grad_part):
    rows = mine_ref.shape[0]
    embed = HEADS * HD
    base = group * SPAN
    row = lax.broadcasted_iota(jnp.int32, bias.shape, 0)
    frame = jnp.where(row < rows, row + place_ref[0 : 1, :], row - rows + place_ref[1 : 2, :])
    bias[...] = jnp.where(frame < length_ref[0, 0], 0.0, -1e30)
    across = (((1,), (1,)), ((), ()))
    downward = (((0,), (0,)), ((), ()))

    def both(block, start, width):
        mine = mine_ref[:, block * embed + base + start : block * embed + base + start + width]
        peer = peer_ref[:, block * SPAN + start : block * SPAN + start + width]
        return jnp.concatenate([mine, peer], axis=0)

    tiles = SPAN // LANES
    totals = [[None] * tiles for _ in range(4)]
    for head in range(GROUP):
        low = head * HD
        tile = low // LANES
        count = (low + HD - 1) // LANES - tile + 1
        width = count * LANES
        start = tile * LANES
        lane = lax.broadcasted_iota(jnp.int32, (2 * rows, width), 1) + start
        here = (lane >= low) & (lane < low + HD)

        def own(value):
            return jnp.where(here, value, jnp.zeros((), BF16))

        query = both(0, start, width)
        key = own(both(1, start, width))
        value = own(both(2, start, width))
        at = base + start
        cot = jnp.concatenate(
            [cot_ref[:, at : at + width], cot_peer_ref[:rows, at : at + width]], axis=0
        )
        scores = lax.dot_general(key, query, across, preferred_element_type=F32)
        scores = scores + jnp.concatenate([bias[...]] * (2 * rows // LANES), axis=1)
        top = jnp.max(scores, axis=0, keepdims=True)
        raised = jnp.exp((scores - top) * SCALE)
        total = jnp.sum(raised, axis=0, keepdims=True)
        probs_bf = (raised * (1.0 / total)).astype(BF16)
        probs = probs_bf.astype(F32)
        grad_probs = lax.dot_general(value, cot, across, preferred_element_type=F32)
        centre = jnp.sum(probs * grad_probs, axis=0, keepdims=True)
        grad_scores = (probs * (grad_probs - centre) * SCALE).astype(BF16)
        results = (
            lax.dot_general(probs_bf[:, :rows], value, downward, preferred_element_type=F32),
            lax.dot_general(grad_scores[:, :rows], key, downward, preferred_element_type=F32),
            jnp.dot(grad_scores[:rows], own(query), preferred_element_type=F32),
            jnp.dot(probs_bf[:rows], own(cot), preferred_element_type=F32),
        )
        for result, kept in zip(results, totals):
            for index in range(count):
                piece = result[:, index * LANES : (index + 1) * LANES]
                held = kept[tile + index]
                kept[tile + index] = piece if held is None else held + piece
    for index in range(tiles):
        lanes = pl.ds(index * LANES, LANES)
        out_part[:, lanes] = totals[0][index].astype(BF16)
        for block in range(3):
            grad_part[block, :, lanes] = totals[block + 1][index].astype(BF16)

def first_group_kernel(
    depth_ref, gated_ref, place_ref, length_ref, mine_ref, peer_ref, cot_ref, cot_peer_ref,
    depth_out, gated_out, out_part, grad_part, bias, sems,
):
    wait = copy_all([(depth_ref, depth_out), (gated_ref, gated_out)], sems)
    attend_group(
        0, place_ref, length_ref, mine_ref, peer_ref, cot_ref, cot_peer_ref, bias, out_part,
        grad_part,
    )
    wait()


def write_group(group, out_part, grad_part, out_ref, grad_ref, sems):
    copies = [(out_part, out_ref.at[:, pl.ds(group * SPAN, SPAN)])]
    for block in range(3):
        at = block * HEADS * HD + group * SPAN
        copies.append((grad_part.at[block], grad_ref.at[:, pl.ds(at, SPAN)]))
    return copy_all(copies, sems.at[group])


def second_group_kernel(
    out_first, grad_first, place_ref, length_ref, mine_ref, peer_ref, cot_ref, cot_peer_ref,
    out_ref, grad_ref, out_part, grad_part, bias, sems,
):
    wait = write_group(0, out_first, grad_first, out_ref, grad_ref, sems)
    attend_group(
        1, place_ref, length_ref, mine_ref, peer_ref, cot_ref, cot_peer_ref, bias, out_part,
        grad_part,
    )
    write_group(1, out_part, grad_part, out_ref, grad_ref, sems)()
    wait()


def attention_call(group, place, length, mine, peer, arriving, cot_peer, earlier):
    rows, columns = mine.shape
    parts = [shaped(rows, SPAN), shaped(3, rows, SPAN)]
    scratch = [pltpu.VMEM((2 * rows, LANES), F32)]
    if group == 0:
        out_shape = [shaped(*value.shape) for value in earlier] + parts
        out_specs = [MEMORY] * 2 + [WHOLE] * 2
        scratch += [pltpu.SemaphoreType.DMA((2,))]
    else:
        out_shape = [shaped(rows, HEADS * HD), shaped(rows, columns)]
        out_specs = [MEMORY] * 2
        scratch = [pltpu.VMEM(part.shape, BF16) for part in parts] + scratch
        scratch += [pltpu.SemaphoreType.DMA((2, 4))]
    return pl.pallas_call(
        (first_group_kernel, second_group_kernel)[group],
        in_specs=[WHOLE] * 3 + [SCALARS] + [WHOLE] * 4,
        out_specs=out_specs,
        out_shape=out_shape,
        scratch_shapes=scratch,
        cost_estimate=pl.CostEstimate(
            flops=PRICE // 64 * 6 * 2 * GROUP * 4 * rows * rows * HD,
            bytes_accessed=2 * rows * 9 * SPAN,
            transcendentals=GROUP * 4 * rows * rows,
        ),
        compiler_params=pltpu.CompilerParams(vmem_limit_bytes=4 * LIMIT),
        name=f"attention_{group}",
    )(*earlier, place, length, mine, peer, arriving, cot_peer)


def head_pass(queries, grad_out, keys_in, values_in, valid_keys):
    query_rows, head_dim = queries.shape
    score_scale = 1.0 / math.sqrt(head_dim)
    block_rows = min(512, query_rows)
    block_count = query_rows // block_rows
    frame_count = keys_in.shape[0]
    across = (((1,), (1,)), ((), ()))
    downward = (((0,), (0,)), ((), ()))

    def advance(totals, blocks):
        query_block, grad_block = blocks
        scores = (
            lax.dot_general(query_block, keys_in, across, preferred_element_type=jnp.float32)
            * score_scale
        )
        scores = jnp.where(valid_keys[None, :], scores, -1e30)
        row_top = jnp.max(scores, axis=1, keepdims=True)
        row_total = jnp.sum(jnp.exp(scores - row_top), axis=1, keepdims=True)
        probs_bf = (jnp.exp(scores - row_top) / row_total).astype(jnp.bfloat16)
        attended_full = jnp.dot(probs_bf, values_in, preferred_element_type=jnp.float32)
        attended = attended_full.astype(jnp.bfloat16)
        grad_probs = lax.dot_general(
            grad_block, values_in, across, preferred_element_type=jnp.float32
        )
        centre = jnp.sum(grad_block.astype(jnp.float32) * attended_full, axis=1, keepdims=True)
        grad_scores = (probs_bf.astype(jnp.float32) * (grad_probs - centre) * score_scale).astype(
            jnp.bfloat16
        )
        grad_query = jnp.dot(grad_scores, keys_in, preferred_element_type=jnp.float32).astype(
            jnp.bfloat16
        )
        key_total = totals[0] + lax.dot_general(
            grad_scores, query_block, downward, preferred_element_type=jnp.float32
        )
        value_total = totals[1] + lax.dot_general(
            probs_bf, grad_block, downward, preferred_element_type=jnp.float32
        )
        return ((key_total, value_total), (attended, grad_query))

    zero_grads = jnp.zeros((frame_count, head_dim), jnp.float32)
    blocked = (
        queries.reshape(block_count, block_rows, head_dim),
        grad_out.reshape(block_count, block_rows, head_dim),
    )
    totals, results = lax.scan(advance, (zero_grads, zero_grads), blocked)
    attended = results[0].reshape(query_rows, head_dim)
    grad_query = results[1].reshape(query_rows, head_dim)
    return (attended, grad_query, totals[0], totals[1])


def attend_block(query_part, grad_part, key_value, valid_keys, heads_dev):
    block_width = heads_dev * HD

    def split_heads(matrix):
        return matrix.reshape(matrix.shape[0], heads_dev, HD).transpose(1, 0, 2)

    def join_heads(matrix):
        return matrix.transpose(1, 0, 2).reshape(matrix.shape[1], block_width)

    def one_head(items):
        return head_pass(items[0], items[1], items[2], items[3], valid_keys)

    stacked = (
        split_heads(query_part),
        split_heads(grad_part),
        split_heads(key_value[:, :block_width]),
        split_heads(key_value[:, block_width:]),
    )
    attended, grad_query, key_grad, value_grad = lax.map(one_head, stacked)
    key_grads = jnp.concatenate([join_heads(key_grad), join_heads(value_grad)], axis=1)
    return (join_heads(attended), join_heads(grad_query), key_grads)


def attend_by_heads(mixed, grad_attn, valid_keys):
    rows_here = mixed.shape[0]
    devices_ctx = lax.axis_size("ctx")
    embed = HEADS * HD
    part_count = max(devices_ctx // HEADS, 1)
    heads_dev = max(HEADS // devices_ctx, 1)
    block_heads = HEADS // heads_dev
    part_rows = rows_here // part_count
    block_width = heads_dev * HD
    queries = mixed[:, :embed]
    keys_in = mixed[:, embed : 2 * embed]
    values_in = mixed[:, 2 * embed :]

    def by_part(matrix):
        split = matrix.reshape(part_count, part_rows, block_heads, block_width).transpose(
            2, 0, 1, 3
        )
        return split.reshape(devices_ctx, part_rows, block_width)

    def swap(value, concat):
        return lax.all_to_all(value, "ctx", split_axis=0, concat_axis=concat, tiled=True)

    key_value = jnp.concatenate(
        [
            keys_in.reshape(rows_here, block_heads, block_width),
            values_in.reshape(rows_here, block_heads, block_width),
        ],
        axis=2,
    )
    key_value = jnp.repeat(key_value.transpose(1, 0, 2), part_count, axis=0)
    query_part = swap(by_part(queries), 1)[0]
    grad_part = swap(by_part(grad_attn), 1)[0]
    key_value = swap(key_value, 1)[0]
    attended, grad_query, key_grads = attend_block(
        query_part, grad_part, key_value, valid_keys, heads_dev
    )
    outgoing = jnp.concatenate([attended, grad_query], axis=1).reshape(
        devices_ctx, part_rows, 2 * block_width
    )
    returned = swap(outgoing, 0)
    key_returned = swap(
        key_grads.reshape(devices_ctx, rows_here, 2 * block_width).astype(BF16), 0
    ).astype(F32)
    columns = 2 * block_width
    split = returned.reshape(block_heads, part_count, part_rows, columns).transpose(1, 2, 0, 3)
    returned = split.reshape(rows_here, block_heads, columns)
    attention_out = returned[:, :, :block_width].reshape(rows_here, embed)
    grad_q = returned[:, :, block_width:].reshape(rows_here, embed)
    summed = jnp.sum(
        key_returned.reshape(block_heads, part_count, rows_here, 2 * block_width), axis=1
    )
    summed = summed.astype(BF16).transpose(1, 0, 2)
    grad_k = summed[:, :, :block_width].reshape(rows_here, embed)
    grad_v = summed[:, :, block_width:].reshape(rows_here, embed)
    return attention_out, jnp.concatenate([grad_q, grad_k, grad_v], axis=1)


def add_kernel(mine_ref, other_ref, out_ref):
    out_ref[...] = (mine_ref[...].astype(F32) + other_ref[...].astype(F32)).astype(BF16)


def last_sum_kernel(mine_ref, other_ref, taps_ref, bias_ref):
    total = mine_ref[...].astype(F32) + other_ref[...].astype(F32)
    for k in range(KSIZE):
        taps_ref[k] = total[k : k + 1]
    bias_ref[...] = total[KSIZE:]


def sum_steps():
    return [
        (axis, 1 << bit)
        for axis in ("dp", "ctx")
        for bit in range(lax.axis_size(axis).bit_length() - 1)
    ]


def exchanged(value, axis, step):
    return lax.ppermute(value, axis, [(i, i ^ step) for i in range(lax.axis_size(axis))])


def add(value, other):
    return pl.pallas_call(
        add_kernel,
        in_specs=[WHOLE] * 2,
        out_specs=WHOLE,
        out_shape=shaped(*value.shape),
        compiler_params=PARAMS,
        name="add",
    )(value, other)


def last_sum(value, other):
    channels = value.shape[1]
    return pl.pallas_call(
        last_sum_kernel,
        in_specs=[WHOLE] * 2,
        out_specs=[WHOLE] * 2,
        out_shape=[shaped(KSIZE, 1, channels, dtype=F32), shaped(1, channels, dtype=F32)],
        compiler_params=PARAMS,
        name="last_sum",
    )(value, other)


def route(pairs, pipe_shift):
    sections, devices = lax.axis_size("pipe"), lax.axis_size("ctx")
    return [
        (s * devices + a, ((s - pipe_shift) % sections) * devices + b)
        for s in range(sections)
        for a, b in pairs
    ]


SWAP = [(0, 1), (1, 0)]


def edges(block, count, pipe_shift):
    rows, devices = block.shape[0], lax.axis_size("ctx")
    upward = [(i, i + 1) for i in range(devices - 1)]
    downward = [(b, a) for a, b in upward]
    low = lax.ppermute(block[rows - count :], ("pipe", "ctx"), route(upward, pipe_shift))
    high = lax.ppermute(block[:count], ("pipe", "ctx"), route(downward, pipe_shift))
    return low, high


def local(projected, gated_input, upstream, lengths, depth_kernel, depth_bias):
    embed = HEADS * HD
    sections, devices = lax.axis_size("pipe"), lax.axis_size("ctx")
    me = lax.axis_index("ctx")
    mixed, gated, sent = projected[0, 0], gated_input[0, 0], upstream[0, 0]
    taps = depth_kernel.reshape(KSIZE, 1, -1)
    rows = mixed.shape[0]
    frames = rows * devices
    first = me * rows
    row = lax.broadcasted_iota(jnp.int32, (8, LANES), 0)
    place = jnp.where(row == 0, first, jnp.where(row == 1, (1 - me) * rows, frames))
    arriving = lax.ppermute(sent, "pipe", [(i, (i - 1) % sections) for i in range(sections)])
    if devices == 2:
        edge, piece, *parts = cut(gated, sent, mixed, 1 - me)
        gated_low = gated_high = lax.ppermute(edge, "ctx", SWAP)
        cot_low = cot_high = cot_peer = lax.ppermute(piece, ("pipe", "ctx"), route(SWAP, 1))
        peers = [lax.ppermute(part, "ctx", SWAP) for part in parts]
    else:
        gated_low, gated_high = edges(gated, EDGE, 0)
        cot_low, cot_high = [
            jnp.concatenate(jnp.split(side, side.shape[1] // embed, axis=1), axis=0)
            for side in edges(sent[:, embed:], SLIM, 1)
        ]
    depth_out, source, slopes = conv_pre(
        place, lengths, gated, gated_low, gated_high, taps, depth_bias
    )
    grads, sums = conv_sums(source, slopes, arriving)
    *steps, last_step = sum_steps()
    for step in steps:
        sums = add(sums, exchanged(sums, *step))
    kernel_grad, bias_grad = last_sum(sums, exchanged(sums, *last_step))
    gated_grad = conv_back(
        place, lengths, source, grads, cot_low, cot_high, taps, depth_bias
    )
    if devices == 2:
        given = (mixed, peers[0], arriving, cot_peer)
        depth_out, gated_grad, *first_results = attention_call(
            0, place, lengths, *given, (depth_out, gated_grad)
        )
        given = (mixed, peers[1], arriving, cot_peer)
        attention_out, projected_grad = attention_call(1, place, lengths, *given, first_results)
    else:
        attention_out, projected_grad = attend_by_heads(
            mixed, arriving[:, :embed], jnp.arange(frames) < lengths[0, 0]
        )
    return (
        attention_out[None, None],
        depth_out[None, None],
        projected_grad[None, None],
        gated_grad[None, None],
        kernel_grad.reshape(1, KSIZE, -1),
        bias_grad,
    )


def solution(mesh):
    by_frame = P("pipe", "dp", "ctx", None)
    return jax.shard_map(
        local,
        mesh=mesh,
        in_specs=(
            by_frame,
            by_frame,
            by_frame,
            P("pipe", "dp"),
            P("pipe", None, None),
            P("pipe", None),
        ),
        out_specs=(
            by_frame,
            by_frame,
            by_frame,
            by_frame,
            P("pipe", None, None),
            P("pipe", None),
        ),
        check_vma=False,
    )
```
